512 devices in a mesh: stn: 64 (over x, z_lo, y), chan: 8 (over z_hi, core).
Axes of the slice: x: 4, y: 4, z: 16 (z_hi: 4, z_lo: 4; z = z_hi * 4 + z_lo), core: 2. Of those that a mesh axis runs over, the one named last changes fastest.
Arguments:
- voltages: bfloat16 [512, 2, 143, 2048], P(('stn', 'chan')), may hold values from -6 to 6
- flags: float32 [256, 128], P('stn'), may hold values from 0 to 1, as said below
- station_row: int32 [256], P('stn'), may hold values from 0 to 255, each once
Outputs:
- visibility: bfloat16 [2048, 512, 512], P(('stn', 'chan'))
The draws below stay inside these ranges and needn't reach their ends.
Inputs may be any that keep to these rules, and one draw needn't show every extreme that they name: `flags`: 0 marks a flagged spectrum of a station, 1 a fully usable one; some stations have 0 at all 128 spectra. `station_row`: every row pair is given to exactly one station.
All inputs are finite; a program needn't handle non-finite values.
Results may differ from the reference program's by a relative error of at most 0.006.
Values may be sent and summed in bfloat16 or wider, within the bound.
No kernel may reach another device: no remote copies, remote signals or barrier semaphores. Data moves between devices by JAX's collectives and lax.ppermute only.
A program may use at most 64 MiB of HBM per device.

```python
import math
import jax
import jax.numpy as jnp
from jax import lax

CH = 2048
TAPS = 16
SPECTRA = 128
INPUTS = 512
STATIONS = 256
FRAMES = 143


def draw_flags(key, part):
    first, second, third, fourth, fifth = jax.random.split(jax.random.fold_in(key, 11), 5)
    level = jax.random.uniform(first, (STATIONS, SPECTRA), jnp.float32, 0.25, 1.0)
    full = jax.random.randint(second, (STATIONS, SPECTRA), 0, 4) == 0
    dropped = jax.random.randint(third, (STATIONS, SPECTRA), 0, 8) == 0
    lost = jax.random.randint(fourth, (STATIONS, 1), 0, 16) == 0
    chosen = jax.random.randint(fifth, (), 0, STATIONS)
    lost = jnp.logical_or(lost, (jnp.arange(STATIONS) == chosen)[:, None])
    value = jnp.where(full, 1.0, level)
    value = jnp.where(dropped, 0.0, value)
    value = jnp.where(lost, 0.0, value)
    return value.astype(jnp.float32)


def shard_levels(stream_key, extent, shards, low, high):
    gain = 1.0
    for axis_at, shards_of in shards:
        steps = jax.random.uniform(jax.random.fold_in(jax.random.fold_in(stream_key, 6), axis_at), (shards_of,), jnp.float32, low / len(shards), high / len(shards))
        gain = gain * jnp.repeat(jnp.exp(steps), extent[axis_at] // shards_of).reshape((-1,) + (1,) * (len(extent) - 1 - axis_at))
    return gain


def centred(own_key, extent, scale, most, cuts=(), kind=jnp.bfloat16):
    factor_of = shard_levels(own_key, extent, cuts, -0.22, 0.18) if cuts else 1.0
    entries = jax.random.normal(own_key, extent, jnp.float32) * scale * factor_of
    return jnp.minimum(jnp.maximum(entries, -most), most).astype(kind)


def setup_inputs(seed: int = 0) -> dict:
    streams_of = jax.random.split(jax.random.key(seed), 4)
    voltages = centred(streams_of[0], (INPUTS, 2, FRAMES, CH), 1.0, 6.0, ((0, 512),))
    flags = draw_flags(jax.random.fold_in(streams_of[3], 71), 0)
    station_row = jax.random.permutation(streams_of[2], STATIONS).astype(jnp.int32)
    return dict(voltages=voltages, flags=flags, station_row=station_row)


def filter_table(taps, lanes):
    total = taps * lanes
    places = jnp.arange(total, dtype=jnp.float32) + 0.5
    window = 0.5 - 0.5 * jnp.cos(2.0 * math.pi * places / total)
    return (jnp.sinc((places - 0.5 * total) / lanes) * window).reshape(taps, lanes)

def reference(voltages, flags, station_row):
    taps_table = filter_table(TAPS, CH)

    def channelize(single):
        samples = single[0].astype(jnp.float32) + 1j * single[1].astype(jnp.float32)
        filtered = taps_table[0] * samples[0:SPECTRA, :]
        for tap_index in range(1, TAPS):
            filtered = filtered + taps_table[tap_index] * samples[tap_index:tap_index + SPECTRA, :]
        spectrum = jnp.fft.fft(filtered, axis=-1) / math.sqrt(CH)
        return jnp.stack([jnp.real(spectrum).astype(jnp.bfloat16), jnp.imag(spectrum).astype(jnp.bfloat16)])
    spectra = lax.map(channelize, voltages)
    order = jnp.argsort(station_row).astype(jnp.int32)
    rows = jnp.arange(INPUTS, dtype=jnp.int32)
    station_of = order[rows // 2]
    source = 2 * station_of + rows % 2
    weights = flags[station_of].astype(jnp.float32)
    kept = (spectra[source].astype(jnp.float32) * weights[:, None, :, None]).astype(jnp.bfloat16)
    stacked = jnp.transpose(kept, (3, 0, 1, 2)).reshape(CH, INPUTS, 2 * SPECTRA)
    rotated = jnp.concatenate([-kept[:, 1], kept[:, 0]], axis=1)
    rotated = jnp.transpose(rotated, (2, 0, 1))
    count = jnp.dot(weights, weights.T, preferred_element_type=jnp.float32, precision=lax.Precision.HIGHEST)
    denom = jnp.maximum(count, 1.0)
    lower = rows[:, None] >= rows[None, :]
    block = 16
    groups = CH // block

    def correlate(pieces):
        plain, turned = pieces
        plain32 = plain.astype(jnp.float32)
        turned32 = turned.astype(jnp.float32)
        real_part = jnp.einsum('cat,cbt->cab', plain32, plain32) / denom
        imag_part = jnp.einsum('cat,cbt->cab', plain32, turned32) / denom
        return jnp.where(lower[None], real_part, imag_part).astype(jnp.bfloat16)
    result = lax.map(correlate, (stacked.reshape(groups, block, INPUTS, 2 * SPECTRA), rotated.reshape(groups, block, INPUTS, 2 * SPECTRA)))
    return result.reshape(CH, INPUTS, INPUTS)
```

```python
import math
import numpy as np
import jax
import jax.numpy as jnp
from jax import lax
from jax.experimental import pallas as pl
from jax.experimental.pallas import tpu as pltpu
from jax.sharding import PartitionSpec as P

F32 = jnp.float32
BF16 = jnp.bfloat16


def filter_rows(taps, lanes):
    total = taps * lanes
    places = np.arange(total, dtype=np.float64) + 0.5
    window = 0.5 - 0.5 * np.cos(2.0 * np.pi * places / total)
    table = np.sinc((places - 0.5 * total) / lanes) * window
    return table.reshape(taps, lanes).astype(np.float32)


def twist_rows(outer, inner):
    k = np.arange(outer)[:, None] * np.arange(inner)[None, :]
    angle = 2.0 * np.pi * k / (outer * inner)
    return np.stack([np.cos(angle), np.sin(angle)]).astype(np.float32)


def inner_matrix(inner, scale):
    jn = np.arange(inner)[:, None] * np.arange(inner)[None, :] % inner
    angle = 2.0 * np.pi * jn / inner
    cos, sin = np.cos(angle) * scale, np.sin(angle) * scale
    real = np.concatenate([cos, sin], axis=1)
    imag = np.concatenate([-sin, cos], axis=1)
    return np.stack([real, imag], axis=1).reshape(2 * inner, 2 * inner)


def small_transform(re, im):
    def four(a, b, c, d):
        (ar, ai), (br, bi), (cr, ci), (dr, di) = a, b, c, d
        pr, pi, qr, qi = ar + cr, ai + ci, ar - cr, ai - ci
        rr, ri, sr, si = br + dr, bi + di, br - dr, bi - di
        return [
            (pr + rr, pi + ri),
            (qr + si, qi - sr),
            (pr - rr, pi - ri),
            (qr - si, qi + sr),
        ]

    x = list(zip(re, im))
    mid = [four(x[b], x[4 + b], x[8 + b], x[12 + b]) for b in range(4)]
    out = [None] * 16
    for p in range(4):
        row = []
        for b in range(4):
            r, i = mid[b][p]
            e = (b * p) % 16
            if e == 0:
                row.append((r, i))
            elif e == 4:
                row.append((i, -r))
            elif e == 2:
                s = math.sqrt(0.5)
                row.append(((r + i) * s, (i - r) * s))
            elif e == 6:
                s = math.sqrt(0.5)
                row.append(((i - r) * s, -(r + i) * s))
            else:
                c, s = math.cos(2 * math.pi * e / 16), math.sin(2 * math.pi * e / 16)
                row.append((r * c + i * s, i * c - r * s))
        done = four(*row)
        for q in range(4):
            out[p + 4 * q] = done[q]
    return out


def channelize_kernel(v_ref, h_ref, tw_ref, dhi_ref, dlo_ref, w_ref, o_ref, xs_ref, f_ref, ahi_ref, alo_ref):
    taps = h_ref.shape[0]
    outer = xs_ref.shape[1]
    spectra = o_ref.shape[2]
    frames = v_ref.shape[1]

    def filt(m, _):
        at = pl.multiple_of(m * 128, 128)
        for c in range(2):
            xs_ref[c, 0, 0:frames, :] = v_ref[c, :, pl.ds(at, 128)].astype(F32)
        rows = [h_ref[k : k + 1, pl.ds(at, 128)] for k in range(taps)]
        for c in range(2):
            for t in range(0, spectra, 8):
                acc = rows[0] * xs_ref[c, 0, t : t + 8, :]
                for k in range(1, taps):
                    acc = acc + rows[k] * xs_ref[c, 0, t + k : t + k + 8, :]
                f_ref[c, m, t : t + 8, :] = acc
        return 0

    lax.fori_loop(0, f_ref.shape[1], filt, 0)

    def mix(tb, _):
        at = pl.multiple_of(tb * 16, 16)
        parts = []
        for half in range(2):
            here = pl.multiple_of(at + 8 * half, 8)
            re = [f_ref[0, m, pl.ds(here, 8), :] for m in range(16)]
            im = [f_ref[1, m, pl.ds(here, 8), :] for m in range(16)]
            out = small_transform(re, im)
            for k in range(16):
                r, i = out[k]
                if k:
                    cos, sin = tw_ref[0, k : k + 1, :], tw_ref[1, k : k + 1, :]
                    r, i = r * cos + i * sin, i * cos - r * sin
                f_ref[0, k, pl.ds(here, 8), :] = r
                f_ref[1, k, pl.ds(here, 8), :] = i
        for k in range(16):
            for c in range(2):
                val = f_ref[c, k, pl.ds(at, 16), :]
                hi = val.astype(BF16)
                ahi_ref[k, pl.ds(at, 16), c * 128 : (c + 1) * 128] = hi
                alo_ref[k, pl.ds(at, 16), c * 128 : (c + 1) * 128] = (val - hi.astype(F32)).astype(BF16)
        return 0

    lax.fori_loop(0, spectra // 16, mix, 0)
    weight = w_ref[0:1, :]

    def turn(k, _):
        def dot(a, b):
            return lax.dot_general(a, b, (((1,), (1,)), ((), ())), preferred_element_type=F32)

        dhi, dlo = dhi_ref[...], dlo_ref[...]
        hi, lo = ahi_ref[k], alo_ref[k]
        out = dot(dhi, hi) + (dot(dhi, lo) + dot(dlo, hi))
        out = out.astype(BF16).astype(F32) * weight
        o_ref[k] = out.astype(BF16)
        return 0

    lax.fori_loop(0, 16, turn, 0)


def channelize(voltages, weight_row, spectra, interpret=False):
    _, frames, lanes = voltages.shape
    taps = frames - spectra + 1
    h = filter_rows(taps, lanes)
    tw = twist_rows(16, 128)
    d = inner_matrix(128, 1.0 / math.sqrt(lanes))
    dhi = jnp.asarray(d.astype(np.float32)).astype(BF16)
    dhi_np = np.asarray(d.astype(np.float32)).astype(jnp.bfloat16)
    dlo_np = (d - dhi_np.astype(np.float64)).astype(np.float32).astype(jnp.bfloat16)
    padded = (frames + 15) // 16 * 16
    return pl.pallas_call(
        channelize_kernel,
        out_shape=jax.ShapeDtypeStruct((16, 256, spectra), BF16),
        scratch_shapes=[
            pltpu.VMEM((2, 1, padded, 128), F32),
            pltpu.VMEM((2, 16, spectra, 128), F32),
            pltpu.VMEM((16, spectra, 256), BF16),
            pltpu.VMEM((16, spectra, 256), BF16),
        ],
        interpret=interpret,
        name="channelize",
    )(voltages, jnp.asarray(h), jnp.asarray(tw), jnp.asarray(dhi_np), jnp.asarray(dlo_np), weight_row)


def correlate_kernel(x_ref, row_ref, flag_ref, o_ref, sel_ref, inv_ref):
    rows = sel_ref.shape[0]

    def nt(a, b):
        return lax.dot_general(a, b, (((1,), (1,)), ((), ())), preferred_element_type=F32)

    @pl.when(pl.program_id(0) == 0)
    def _():
        at = lax.broadcasted_iota(jnp.int32, (rows, rows), 0)
        sel = jnp.where(row_ref[0:1, :] == at, 1.0, 0.0).astype(BF16)
        sel_ref[...] = sel
        flag = flag_ref[...]
        hi = flag.astype(BF16)
        rest = flag - hi.astype(F32)
        mid = rest.astype(BF16)
        low = (rest - mid.astype(F32)).astype(BF16)
        pieces = jnp.concatenate([hi, mid, low], axis=1)
        placed = jnp.dot(sel, pieces, preferred_element_type=F32).astype(BF16)
        n = flag.shape[1]
        hi, mid, low = placed[:, :n], placed[:, n : 2 * n], placed[:, 2 * n :]
        left = jnp.concatenate([hi, hi, mid, mid, hi, low], axis=1)
        right = jnp.concatenate([hi, mid, hi, mid, low, hi], axis=1)
        count = nt(left, right)
        inv_ref[...] = 1.0 / jnp.maximum(count, 1.0)

    kept = jnp.dot(sel_ref[...], x_ref[0], preferred_element_type=F32)
    half = kept.shape[1] // 2
    plain = kept.astype(BF16)
    turned = jnp.concatenate([-kept[:, half:], kept[:, :half]], axis=1).astype(BF16)
    n = rows // 2
    for a in range(2):
        for b in range(2):
            pa = plain[a * n : (a + 1) * n]
            if a > b:
                out = nt(pa, plain[b * n : (b + 1) * n])
            elif a < b:
                out = nt(pa, turned[b * n : (b + 1) * n])
            else:
                real = nt(pa, pa)
                imag = nt(pa, turned[b * n : (b + 1) * n])
                below = lax.broadcasted_iota(jnp.int32, (n, n), 0) >= lax.broadcasted_iota(jnp.int32, (n, n), 1)
                out = jnp.where(below, real, imag)
            inv = inv_ref[a * n : (a + 1) * n, b * n : (b + 1) * n]
            o_ref[0, a * n : (a + 1) * n, b * n : (b + 1) * n] = (out * inv).astype(BF16)


def correlate(arrived, row_of, flags, interpret=False):
    channels, inputs, wide = arrived.shape
    return pl.pallas_call(
        correlate_kernel,
        grid=(channels,),
        in_specs=[
            pl.BlockSpec((1, inputs, wide), lambda i: (i, 0, 0)),
            pl.BlockSpec(row_of.shape, lambda i: (0, 0)),
            pl.BlockSpec(flags.shape, lambda i: (0, 0)),
        ],
        out_specs=pl.BlockSpec((1, inputs, inputs), lambda i: (i, 0, 0)),
        out_shape=jax.ShapeDtypeStruct((channels, inputs, inputs), BF16),
        scratch_shapes=[pltpu.VMEM((inputs, inputs), BF16), pltpu.VMEM((inputs, inputs), F32)],
        interpret=interpret,
        name="correlate",
    )(arrived, row_of, flags)


def gather_flags(flags, station_row):
    own = flags.shape[0]
    tile = jnp.concatenate(
        [flags, jnp.broadcast_to(station_row.astype(F32)[:, None], flags.shape)], axis=0
    )
    for axes, count in ((("x", "y"), 16), (("l",), 4)):
        tile = jnp.broadcast_to(tile[None], (count,) + tile.shape)
        tile = lax.all_to_all(tile, axes, split_axis=0, concat_axis=0, tiled=True)
    tile = tile.reshape(4, 4, 4, 2, own, flags.shape[1])
    return tile[..., 0, :, :], tile[..., 1, :, 0].astype(jnp.int32)


def on_device(voltages, flags, station_row):
    spectra = flags.shape[1]
    z_hi = 2 * lax.axis_index("a") + lax.axis_index("b")
    flags_all, rows_all = gather_flags(flags, station_row)
    weight = lax.dynamic_slice_in_dim(flags, z_hi, 1, 0)
    weight = jnp.broadcast_to(weight, (8, spectra))
    made = channelize(voltages[0], weight, spectra)
    grid = made.reshape(2, 2, 4, 4, 4, 4, 2, 2, spectra)
    blocks = jnp.transpose(grid, (3, 5, 6, 0, 4, 1, 2, 7, 8)).reshape(512, 8, spectra)
    moved = lax.all_to_all(blocks, ("x", "y", "a", "b", "l", "c"), split_axis=0, concat_axis=0, tiled=True)
    arrived = jnp.transpose(moved.reshape(512, 4, 2 * spectra), (1, 0, 2))
    flag_src = jnp.transpose(flags_all, (1, 2, 3, 0, 4)).reshape(256, 1, spectra)
    flag_src = jnp.broadcast_to(flag_src, (256, 2, spectra)).reshape(512, spectra)
    row_src = 2 * jnp.transpose(rows_all, (1, 2, 3, 0)).reshape(256, 1) + jnp.arange(2, dtype=jnp.int32)[None]
    row_src = jnp.broadcast_to(row_src.reshape(1, 512), (8, 512))
    return correlate(arrived, row_src, flag_src)


def solution(mesh):
    axes = ("x", "l", "y", "a", "b", "c")
    fine = jax.sharding.Mesh(mesh.devices.reshape(4, 4, 4, 2, 2, 2), axes)
    stn = axes[:3]
    return jax.shard_map(
        on_device,
        mesh=fine,
        in_specs=(P(axes, None, None, None), P(stn, None), P(stn)),
        out_specs=P(axes, None, None),
        check_vma=False,
    )
```

```python
import math
import numpy as np
import jax
import jax.numpy as jnp
from jax import lax
from jax.experimental import pallas as pl
from jax.experimental.pallas import tpu as pltpu
from jax.sharding import PartitionSpec as P

F32 = jnp.float32
BF16 = jnp.bfloat16


def filter_rows(taps, lanes):
    total = taps * lanes
    places = np.arange(total, dtype=np.float64) + 0.5
    window = 0.5 - 0.5 * np.cos(2.0 * np.pi * places / total)
    table = np.sinc((places - 0.5 * total) / lanes) * window
    return table.reshape(taps, lanes).astype(np.float32)


def twist_rows(outer, inner):
    k = np.arange(outer)[:, None] * np.arange(inner)[None, :]
    angle = 2.0 * np.pi * k / (outer * inner)
    return np.stack([np.cos(angle), np.sin(angle)]).astype(np.float32)


def inner_matrix(inner, scale):
    jn = np.arange(inner)[:, None] * np.arange(inner)[None, :] % inner
    angle = 2.0 * np.pi * jn / inner
    cos, sin = np.cos(angle) * scale, np.sin(angle) * scale
    real = np.concatenate([cos, sin], axis=1)
    imag = np.concatenate([-sin, cos], axis=1)
    return np.stack([real, imag], axis=1).reshape(2 * inner, 2 * inner)


def small_transform(re, im):
    def four(a, b, c, d):
        (ar, ai), (br, bi), (cr, ci), (dr, di) = a, b, c, d
        pr, pi, qr, qi = ar + cr, ai + ci, ar - cr, ai - ci
        rr, ri, sr, si = br + dr, bi + di, br - dr, bi - di
        return [
            (pr + rr, pi + ri),
            (qr + si, qi - sr),
            (pr - rr, pi - ri),
            (qr - si, qi + sr),
        ]

    x = list(zip(re, im))
    mid = [four(x[b], x[4 + b], x[8 + b], x[12 + b]) for b in range(4)]
    out = [None] * 16
    for p in range(4):
        row = []
        for b in range(4):
            r, i = mid[b][p]
            e = (b * p) % 16
            if e == 0:
                row.append((r, i))
            elif e == 4:
                row.append((i, -r))
            elif e == 2:
                s = math.sqrt(0.5)
                row.append(((r + i) * s, (i - r) * s))
            elif e == 6:
                s = math.sqrt(0.5)
                row.append(((i - r) * s, -(r + i) * s))
            else:
                c, s = math.cos(2 * math.pi * e / 16), math.sin(2 * math.pi * e / 16)
                row.append((r * c + i * s, i * c - r * s))
        done = four(*row)
        for q in range(4):
            out[p + 4 * q] = done[q]
    return out


def channelize_kernel(v_ref, h_ref, tw_ref, dhi_ref, dlo_ref, w_ref, z_ref, o_ref, xs_ref, f_ref, ahi_ref, alo_ref, m_ref):
    taps = h_ref.shape[0]
    frames = v_ref.shape[0]
    spectra = w_ref.shape[1]

    def filt(m, _):
        at = pl.multiple_of(m * 128, 128)
        for c in range(2):
            xs_ref[c, 0:frames, :] = v_ref[:, c, pl.ds(at, 128)].astype(F32)
        rows = [h_ref[k : k + 1, pl.ds(at, 128)] for k in range(taps)]
        for c in range(2):
            for t in range(0, spectra, 8):
                acc = rows[0] * xs_ref[c, t : t + 8, :]
                for k in range(1, taps):
                    acc = acc + rows[k] * xs_ref[c, t + k : t + k + 8, :]
                f_ref[c, m, t : t + 8, :] = acc
        return 0

    lax.fori_loop(0, f_ref.shape[1], filt, 0)

    def mix(tb, _):
        at = pl.multiple_of(tb * 16, 16)
        for half in range(2):
            here = pl.multiple_of(at + 8 * half, 8)
            re = [f_ref[0, m, pl.ds(here, 8), :] for m in range(16)]
            im = [f_ref[1, m, pl.ds(here, 8), :] for m in range(16)]
            out = small_transform(re, im)
            for k in range(16):
                r, i = out[k]
                if k:
                    cos, sin = tw_ref[0, k : k + 1, :], tw_ref[1, k : k + 1, :]
                    r, i = r * cos + i * sin, i * cos - r * sin
                f_ref[0, k, pl.ds(here, 8), :] = r
                f_ref[1, k, pl.ds(here, 8), :] = i
        for k in range(16):
            for c in range(2):
                val = f_ref[c, k, pl.ds(at, 16), :]
                hi = val.astype(BF16)
                ahi_ref[k, pl.ds(at, 16), c * 128 : (c + 1) * 128] = hi
                alo_ref[k, pl.ds(at, 16), c * 128 : (c + 1) * 128] = (val - hi.astype(F32)).astype(BF16)
        return 0

    lax.fori_loop(0, spectra // 16, mix, 0)

    def turn(q, _):
        def dot(a, b):
            return lax.dot_general(a, b, (((1,), (1,)), ((), ())), preferred_element_type=F32)

        weight = w_ref[pl.ds(z_ref[0], 1), :]
        dhi, dlo = dhi_ref[...], dlo_ref[...]
        for i in range(4):
            hi, lo = ahi_ref[4 * q + i], alo_ref[4 * q + i]
            out = dot(dhi, hi) + (dot(dhi, lo) + dot(dlo, hi))
            out = out.astype(BF16).astype(F32) * weight
            for c in range(2):
                m_ref[pl.ds(2 * i + c, 128, stride=8), :] = out[128 * c : 128 * (c + 1)]
        o_ref[pl.ds(pl.multiple_of(q * 1024, 1024), 1024), :] = m_ref[...].astype(BF16)
        return 0

    lax.fori_loop(0, 4, turn, 0)


def channelize(voltages, flags, station, spectra, interpret=False):
    frames, _, lanes = voltages.shape
    taps = frames - spectra + 1
    h = filter_rows(taps, lanes)
    tw = twist_rows(16, 128)
    d = inner_matrix(128, 1.0 / math.sqrt(lanes))
    d = d.reshape(4, 4, 4, 2, 2, 256).transpose(4, 0, 2, 3, 1, 5).reshape(256, 256)
    dhi = d.astype(np.float32).astype(jnp.bfloat16)
    dlo = (d - dhi.astype(np.float64)).astype(np.float32).astype(jnp.bfloat16)
    padded = (frames + 7) // 8 * 8
    return pl.pallas_call(
        channelize_kernel,
        out_shape=jax.ShapeDtypeStruct((4096, spectra), BF16),
        scratch_shapes=[
            pltpu.VMEM((2, padded, 128), F32),
            pltpu.VMEM((2, 16, spectra, 128), F32),
            pltpu.VMEM((16, spectra, 256), BF16),
            pltpu.VMEM((16, spectra, 256), BF16),
            pltpu.VMEM((1024, spectra), F32),
        ],
        in_specs=[pl.BlockSpec(memory_space=pltpu.VMEM)] * 6 + [pl.BlockSpec(memory_space=pltpu.SMEM)],
        interpret=interpret,
        name="channelize",
    )(voltages, jnp.asarray(h), jnp.asarray(tw), jnp.asarray(dhi), jnp.asarray(dlo), flags, station)


def correlate_kernel(x_ref, row_ref, flag_ref, o_ref, sel_ref, inv_ref, s_ref):
    rows = sel_ref.shape[0]

    def nt(a, b):
        return lax.dot_general(a, b, (((1,), (1,)), ((), ())), preferred_element_type=F32)

    @pl.when(pl.program_id(0) == 0)
    def _():
        at = lax.broadcasted_iota(jnp.int32, (rows, rows), 0)
        sel = jnp.where(row_ref[0:1, :] == at, 1.0, 0.0).astype(BF16)
        sel_ref[...] = sel
        flag = flag_ref[...]
        hi = flag.astype(BF16)
        rest = flag - hi.astype(F32)
        mid = rest.astype(BF16)
        low = (rest - mid.astype(F32)).astype(BF16)
        pieces = jnp.concatenate([hi, mid, low], axis=1)
        placed = jnp.dot(sel, pieces, preferred_element_type=F32).astype(BF16)
        n = flag.shape[1]
        hi, mid, low = placed[:, :n], placed[:, n : 2 * n], placed[:, 2 * n :]
        left = jnp.concatenate([hi, hi, mid, mid, hi, low], axis=1)
        right = jnp.concatenate([hi, mid, hi, mid, low, hi], axis=1)
        count = nt(left, right)
        inv_ref[...] = 1.0 / jnp.maximum(count, 1.0)
        s_ref[...] = x_ref[...].astype(F32)

    at = 2 * pl.program_id(0)
    mine = jnp.concatenate([s_ref[pl.ds(at, rows, stride=8), :], s_ref[pl.ds(at + 1, rows, stride=8), :]], axis=1)
    kept = jnp.dot(sel_ref[...], mine.astype(BF16), preferred_element_type=F32)
    half = kept.shape[1] // 2
    plain = kept.astype(BF16)
    turned = jnp.concatenate([-kept[:, half:], kept[:, :half]], axis=1).astype(BF16)
    n = rows // 2
    for a in range(2):
        for b in range(2):
            pa = plain[a * n : (a + 1) * n]
            if a > b:
                out = nt(pa, plain[b * n : (b + 1) * n])
            elif a < b:
                out = nt(pa, turned[b * n : (b + 1) * n])
            else:
                real = nt(pa, pa)
                imag = nt(pa, turned[b * n : (b + 1) * n])
                below = lax.broadcasted_iota(jnp.int32, (n, n), 0) >= lax.broadcasted_iota(jnp.int32, (n, n), 1)
                out = jnp.where(below, real, imag)
            inv = inv_ref[a * n : (a + 1) * n, b * n : (b + 1) * n]
            o_ref[0, a * n : (a + 1) * n, b * n : (b + 1) * n] = (out * inv).astype(BF16)


def correlate(arrived, row_of, flags, interpret=False):
    channels, inputs = 4, flags.shape[0]
    return pl.pallas_call(
        correlate_kernel,
        grid=(channels,),
        in_specs=[
            pl.BlockSpec(arrived.shape, lambda i: (0, 0)),
            pl.BlockSpec(row_of.shape, lambda i: (0, 0)),
            pl.BlockSpec(flags.shape, lambda i: (0, 0)),
        ],
        out_specs=pl.BlockSpec((1, inputs, inputs), lambda i: (i, 0, 0)),
        out_shape=jax.ShapeDtypeStruct((channels, inputs, inputs), BF16),
        scratch_shapes=[
            pltpu.VMEM((inputs, inputs), BF16),
            pltpu.VMEM((inputs, inputs), F32),
            pltpu.VMEM(arrived.shape, F32),
        ],
        interpret=interpret,
        name="correlate",
    )(arrived, row_of, flags)


def gather_flags(flags, station_row):
    own = flags.shape[0]
    tile = jnp.concatenate([flags, jnp.broadcast_to(station_row.astype(F32)[:, None], flags.shape)], axis=0)
    tile = jnp.broadcast_to(tile[None], (64,) + tile.shape)
    tile = lax.all_to_all(tile, ("x", "l", "y"), split_axis=0, concat_axis=0, tiled=True)
    return tile.reshape(4, 4, 4, 2, own, flags.shape[1])


def on_device(voltages, flags, station_row):
    spectra = flags.shape[1]
    z_hi = 2 * lax.axis_index("a") + lax.axis_index("b")
    tiles = gather_flags(flags, station_row)
    blocks = channelize(
        jnp.transpose(voltages[0], (1, 0, 2)), flags, z_hi.astype(jnp.int32).reshape(1), spectra
    ).reshape(512, 8, spectra)
    parts = tiles.reshape(4, 4, 4, 2, 2, 2, spectra).transpose(3, 5, 0, 2, 4, 1, 6)
    flag_src = jnp.broadcast_to(parts[0].reshape(2, 1, 128, spectra), (2, 2, 128, spectra)).reshape(512, spectra)
    row_src = parts[1, ..., 0].astype(jnp.int32).reshape(2, 1, 128)
    row_src = (2 * row_src + jnp.arange(2, dtype=jnp.int32)[None, :, None]).reshape(1, 512)
    blocks, flag_src, row_src = lax.optimization_barrier((blocks, flag_src, row_src))
    moved = lax.all_to_all(blocks, ("b", "c", "x", "y", "a", "l"), split_axis=0, concat_axis=0, tiled=True)
    return correlate(moved.reshape(4096, spectra), row_src, flag_src)


def solution(mesh):
    axes = ("x", "l", "y", "a", "b", "c")
    fine = jax.sharding.Mesh(mesh.devices.reshape(4, 4, 4, 2, 2, 2), axes)
    stn = axes[:3]
    return jax.shard_map(
        on_device,
        mesh=fine,
        in_specs=(P(axes, None, None, None), P(stn, None), P(stn)),
        out_specs=P(axes, None, None),
        check_vma=False,
    )
```

```python
import math
import numpy as np
import jax
import jax.numpy as jnp
from jax import lax
from jax.experimental import pallas as pl
from jax.experimental.pallas import tpu as pltpu
from jax.sharding import PartitionSpec as P

F32 = jnp.float32
BF16 = jnp.bfloat16


def filter_rows(taps, lanes):
    total = taps * lanes
    places = np.arange(total, dtype=np.float64) + 0.5
    window = 0.5 - 0.5 * np.cos(2.0 * np.pi * places / total)
    table = np.sinc((places - 0.5 * total) / lanes) * window
    return table.reshape(taps, lanes).astype(np.float32)


def twist_rows(outer, inner):
    k = np.arange(outer)[:, None] * np.arange(inner)[None, :]
    angle = 2.0 * np.pi * k / (outer * inner)
    return np.stack([np.cos(angle), np.sin(angle)]).astype(np.float32)


def inner_matrix(inner, scale):
    jn = np.arange(inner)[:, None] * np.arange(inner)[None, :] % inner
    angle = 2.0 * np.pi * jn / inner
    cos, sin = np.cos(angle) * scale, np.sin(angle) * scale
    real = np.concatenate([cos, sin], axis=1)
    imag = np.concatenate([-sin, cos], axis=1)
    return np.stack([real, imag], axis=1).reshape(2 * inner, 2 * inner)


def small_transform(re, im):
    def four(a, b, c, d):
        (ar, ai), (br, bi), (cr, ci), (dr, di) = a, b, c, d
        pr, pi, qr, qi = ar + cr, ai + ci, ar - cr, ai - ci
        rr, ri, sr, si = br + dr, bi + di, br - dr, bi - di
        return [
            (pr + rr, pi + ri),
            (qr + si, qi - sr),
            (pr - rr, pi - ri),
            (qr - si, qi + sr),
        ]

    x = list(zip(re, im))
    mid = [four(x[b], x[4 + b], x[8 + b], x[12 + b]) for b in range(4)]
    out = [None] * 16
    for p in range(4):
        row = []
        for b in range(4):
            r, i = mid[b][p]
            e = (b * p) % 16
            if e == 0:
                row.append((r, i))
            elif e == 4:
                row.append((i, -r))
            elif e == 2:
                s = math.sqrt(0.5)
                row.append(((r + i) * s, (i - r) * s))
            elif e == 6:
                s = math.sqrt(0.5)
                row.append(((i - r) * s, -(r + i) * s))
            else:
                c, s = math.cos(2 * math.pi * e / 16), math.sin(2 * math.pi * e / 16)
                row.append((r * c + i * s, i * c - r * s))
        done = four(*row)
        for q in range(4):
            out[p + 4 * q] = done[q]
    return out


def channelize_kernel(v_ref, h_ref, tw_ref, dhi_ref, dlo_ref, w_ref, z_ref, o_ref, xs_ref, f_ref, ahi_ref, alo_ref, m_ref):
    taps = h_ref.shape[0]
    frames = v_ref.shape[0]
    spectra = w_ref.shape[1]

    def filt(m, _):
        at = pl.multiple_of(m * 128, 128)
        for c in range(2):
            xs_ref[c, 0:frames, :] = v_ref[:, c, pl.ds(at, 128)].astype(F32)
        rows = [h_ref[k : k + 1, pl.ds(at, 128)] for k in range(taps)]
        for c in range(2):
            for t in range(0, spectra, 8):
                acc = rows[0] * xs_ref[c, t : t + 8, :]
                for k in range(1, taps):
                    acc = acc + rows[k] * xs_ref[c, t + k : t + k + 8, :]
                f_ref[c, m, t : t + 8, :] = acc
        return 0

    lax.fori_loop(0, f_ref.shape[1], filt, 0)

    def mix(tb, _):
        at = pl.multiple_of(tb * 16, 16)
        for half in range(2):
            here = pl.multiple_of(at + 8 * half, 8)
            re = [f_ref[0, m, pl.ds(here, 8), :] for m in range(16)]
            im = [f_ref[1, m, pl.ds(here, 8), :] for m in range(16)]
            out = small_transform(re, im)
            for k in range(16):
                r, i = out[k]
                if k:
                    cos, sin = tw_ref[0, k : k + 1, :], tw_ref[1, k : k + 1, :]
                    r, i = r * cos + i * sin, i * cos - r * sin
                f_ref[0, k, pl.ds(here, 8), :] = r
                f_ref[1, k, pl.ds(here, 8), :] = i
        for k in range(16):
            for c in range(2):
                val = f_ref[c, k, pl.ds(at, 16), :]
                hi = val.astype(BF16)
                ahi_ref[k, pl.ds(at, 16), c * 128 : (c + 1) * 128] = hi
                alo_ref[k, pl.ds(at, 16), c * 128 : (c + 1) * 128] = (val - hi.astype(F32)).astype(BF16)
        return 0

    lax.fori_loop(0, spectra // 16, mix, 0)

    def turn(q, _):
        def dot(a, b):
            return lax.dot_general(a, b, (((1,), (1,)), ((), ())), preferred_element_type=F32)

        weight = w_ref[pl.ds(z_ref[0], 1), :]
        dhi, dlo = dhi_ref[...], dlo_ref[...]
        for i in range(4):
            hi, lo = ahi_ref[4 * q + i], alo_ref[4 * q + i]
            out = dot(dhi, hi) + (dot(dhi, lo) + dot(dlo, hi))
            out = out.astype(BF16).astype(F32) * weight
            for c in range(2):
                m_ref[pl.ds(2 * i + c, 128, stride=8), :] = out[128 * c : 128 * (c + 1)]
        o_ref[pl.ds(pl.multiple_of(q * 1024, 1024), 1024), :] = m_ref[...].astype(BF16)
        return 0

    lax.fori_loop(0, 4, turn, 0)


def channelize(voltages, flags, station, spectra, interpret=False):
    frames, _, lanes = voltages.shape
    taps = frames - spectra + 1
    h = filter_rows(taps, lanes)
    tw = twist_rows(16, 128)
    d = inner_matrix(128, 1.0 / math.sqrt(lanes))
    d = d.reshape(4, 4, 4, 2, 2, 256).transpose(4, 0, 2, 3, 1, 5).reshape(256, 256)
    dhi = d.astype(np.float32).astype(jnp.bfloat16)
    dlo = (d - dhi.astype(np.float64)).astype(np.float32).astype(jnp.bfloat16)
    padded = (frames + 7) // 8 * 8
    return pl.pallas_call(
        channelize_kernel,
        out_shape=jax.ShapeDtypeStruct((4096, spectra), BF16),
        scratch_shapes=[
            pltpu.VMEM((2, padded, 128), F32),
            pltpu.VMEM((2, 16, spectra, 128), F32),
            pltpu.VMEM((16, spectra, 256), BF16),
            pltpu.VMEM((16, spectra, 256), BF16),
            pltpu.VMEM((1024, spectra), F32),
        ],
        in_specs=[pl.BlockSpec(memory_space=pltpu.VMEM)] * 6 + [pl.BlockSpec(memory_space=pltpu.SMEM)],
        interpret=interpret,
        name="channelize",
    )(voltages, jnp.asarray(h), jnp.asarray(tw), jnp.asarray(dhi), jnp.asarray(dlo), flags, station)


def nt(a, b):
    return lax.dot_general(a, b, (((1,), (1,)), ((), ())), preferred_element_type=F32)


def prepare_kernel(tile_ref, sel_ref, inv_ref):
    rows = sel_ref.shape[0]
    tile = tile_ref[...]
    n = tile.shape[1]
    ids = jnp.transpose(tile)[0:8, :]
    ids = jnp.concatenate([ids[:, 4:], ids[:, :4]], axis=1)
    lane = lax.broadcasted_iota(jnp.int32, (8, rows), 1)
    ids = jnp.where((lane & 7) < 4, ids, -1.0)
    down = lax.broadcasted_iota(jnp.int32, (rows, rows), 0)
    pol = (lane >> 7) & 1
    spot = ((lane >> 3) & 15) * 32 + (lane & 3) * 8 + ((lane >> 2) & 1) * 2 + (lane >> 8)
    move = jnp.where(down == spot[0:1], 1.0, 0.0).astype(BF16)
    moved = jnp.dot(ids.astype(BF16), move, preferred_element_type=F32).astype(jnp.int32)
    source_row = 2 * moved + pol
    sel_ref[...] = jnp.where(down == source_row[0:1], 1.0, 0.0).astype(BF16)
    pick = jnp.where((down >> 1) == ids[0:1].astype(jnp.int32), 1.0, 0.0).astype(BF16)
    hi = tile.astype(BF16)
    rest = tile - hi.astype(F32)
    mid = rest.astype(BF16)
    low = (rest - mid.astype(F32)).astype(BF16)
    placed = jnp.dot(pick, jnp.concatenate([hi, mid, low], axis=1), preferred_element_type=F32).astype(BF16)
    hi, mid, low = placed[:, :n], placed[:, n : 2 * n], placed[:, 2 * n :]
    left = jnp.concatenate([hi, hi, mid, mid, hi, low], axis=1)
    right = jnp.concatenate([hi, mid, hi, mid, low, hi], axis=1)
    inv_ref[...] = 1.0 / jnp.maximum(nt(left, right), 1.0)


def prepare(tile, inputs, interpret=False):
    return pl.pallas_call(
        prepare_kernel,
        out_shape=(jax.ShapeDtypeStruct((inputs, inputs), BF16), jax.ShapeDtypeStruct((inputs, inputs), F32)),
        interpret=interpret,
        name="prepare",
    )(tile)


def correlate_kernel(x_ref, sel_ref, inv_ref, o_ref, s_ref):
    rows = sel_ref.shape[0]

    @pl.when(pl.program_id(0) == 0)
    def _():
        s_ref[...] = x_ref[...].astype(F32)

    at = 2 * pl.program_id(0)
    mine = jnp.concatenate([s_ref[pl.ds(at, rows, stride=8), :], s_ref[pl.ds(at + 1, rows, stride=8), :]], axis=1)
    kept = jnp.dot(sel_ref[...], mine.astype(BF16), preferred_element_type=F32)
    half = kept.shape[1] // 2
    plain = kept.astype(BF16)
    turned = jnp.concatenate([-kept[:, half:], kept[:, :half]], axis=1).astype(BF16)
    n = rows // 2
    for a in range(2):
        for b in range(2):
            pa = plain[a * n : (a + 1) * n]
            if a > b:
                out = nt(pa, plain[b * n : (b + 1) * n])
            elif a < b:
                out = nt(pa, turned[b * n : (b + 1) * n])
            else:
                real = nt(pa, pa)
                imag = nt(pa, turned[b * n : (b + 1) * n])
                below = lax.broadcasted_iota(jnp.int32, (n, n), 0) >= lax.broadcasted_iota(jnp.int32, (n, n), 1)
                out = jnp.where(below, real, imag)
            inv = inv_ref[a * n : (a + 1) * n, b * n : (b + 1) * n]
            o_ref[0, a * n : (a + 1) * n, b * n : (b + 1) * n] = (out * inv).astype(BF16)


def correlate(arrived, sel, inv, interpret=False):
    inputs = sel.shape[0]
    channels = arrived.shape[0] // (2 * inputs)
    return pl.pallas_call(
        correlate_kernel,
        grid=(channels,),
        in_specs=[pl.BlockSpec(x.shape, lambda i: (0, 0)) for x in (arrived, sel, inv)],
        out_specs=pl.BlockSpec((1, inputs, inputs), lambda i: (i, 0, 0)),
        out_shape=jax.ShapeDtypeStruct((channels, inputs, inputs), BF16),
        scratch_shapes=[pltpu.VMEM(arrived.shape, F32)],
        interpret=interpret,
        name="correlate",
    )(arrived, sel, inv)


def on_device(voltages, flags, station_row):
    spectra = flags.shape[1]
    z_hi = (2 * lax.axis_index("a") + lax.axis_index("b")).astype(jnp.int32).reshape(1)
    tile = jnp.concatenate([flags, jnp.broadcast_to(station_row.astype(F32)[:, None], flags.shape)], axis=0)
    tile = jnp.broadcast_to(tile[None], (64,) + tile.shape)
    tile = lax.all_to_all(tile, ("x", "y", "l"), split_axis=0, concat_axis=0, tiled=True)
    blocks = channelize(jnp.transpose(voltages[0], (1, 0, 2)), flags, z_hi, spectra).reshape(512, 8, spectra)
    moved = lax.all_to_all(blocks, ("b", "c", "x", "y", "a", "l"), split_axis=0, concat_axis=0, tiled=True)
    sel, inv = prepare(tile.reshape(512, spectra), 512)
    return correlate(moved.reshape(4096, spectra), sel, inv)


def solution(mesh):
    axes = ("x", "l", "y", "a", "b", "c")
    fine = jax.sharding.Mesh(mesh.devices.reshape(4, 4, 4, 2, 2, 2), axes)
    stn = axes[:3]
    return jax.shard_map(
        on_device,
        mesh=fine,
        in_specs=(P(axes, None, None, None), P(stn, None), P(stn)),
        out_specs=P(axes, None, None),
        check_vma=False,
    )
```

```python
import math
import numpy as np
import jax
import jax.numpy as jnp
from jax import lax
from jax.experimental import pallas as pl
from jax.experimental.pallas import tpu as pltpu
from jax.sharding import PartitionSpec as P

F32 = jnp.float32
BF16 = jnp.bfloat16


def filter_rows(taps, lanes):
    total = taps * lanes
    places = np.arange(total, dtype=np.float64) + 0.5
    window = 0.5 - 0.5 * np.cos(2.0 * np.pi * places / total)
    table = np.sinc((places - 0.5 * total) / lanes) * window
    return table.reshape(taps, lanes).astype(np.float32)


def twist_rows(outer, inner):
    k = np.arange(outer)[:, None] * np.arange(inner)[None, :]
    angle = 2.0 * np.pi * k / (outer * inner)
    return np.stack([np.cos(angle), np.sin(angle)]).astype(np.float32)


def inner_matrix(inner, scale):
    jn = np.arange(inner)[:, None] * np.arange(inner)[None, :] % inner
    angle = 2.0 * np.pi * jn / inner
    cos, sin = np.cos(angle) * scale, np.sin(angle) * scale
    real = np.concatenate([cos, sin], axis=1)
    imag = np.concatenate([-sin, cos], axis=1)
    return np.stack([real, imag], axis=1).reshape(2 * inner, 2 * inner)


def small_transform(re, im):
    def four(a, b, c, d):
        (ar, ai), (br, bi), (cr, ci), (dr, di) = a, b, c, d
        pr, pi, qr, qi = ar + cr, ai + ci, ar - cr, ai - ci
        rr, ri, sr, si = br + dr, bi + di, br - dr, bi - di
        return [
            (pr + rr, pi + ri),
            (qr + si, qi - sr),
            (pr - rr, pi - ri),
            (qr - si, qi + sr),
        ]

    x = list(zip(re, im))
    mid = [four(x[b], x[4 + b], x[8 + b], x[12 + b]) for b in range(4)]
    out = [None] * 16
    for p in range(4):
        row = []
        for b in range(4):
            r, i = mid[b][p]
            e = (b * p) % 16
            if e == 0:
                row.append((r, i))
            elif e == 4:
                row.append((i, -r))
            elif e == 2:
                s = math.sqrt(0.5)
                row.append(((r + i) * s, (i - r) * s))
            elif e == 6:
                s = math.sqrt(0.5)
                row.append(((i - r) * s, -(r + i) * s))
            else:
                c, s = math.cos(2 * math.pi * e / 16), math.sin(2 * math.pi * e / 16)
                row.append((r * c + i * s, i * c - r * s))
        done = four(*row)
        for q in range(4):
            out[p + 4 * q] = done[q]
    return out


def channelize_kernel(v_ref, h_ref, tw_ref, dhi_ref, dlo_ref, w_ref, z_ref, o_ref, x_ref, f_ref, g_ref, ahi_ref, alo_ref, m_ref):
    taps = h_ref.shape[0] // 32
    spectra = w_ref.shape[1]

    def widen(f, _):
        at = pl.multiple_of(f * 352, 352)
        x_ref[pl.ds(at, 352), :] = v_ref[pl.ds(at, 352), :].astype(F32)
        return 0

    lax.fori_loop(0, x_ref.shape[0] // 352, widen, 0)
    pitch = f_ref.shape[0] // spectra
    step = 16

    for g in range(0, 32, 8):

        def filt(tb, _):
            first = tb * step
            rows = [h_ref[32 * k + g : 32 * k + g + 8, :] for k in range(taps)]
            x = [x_ref[pl.ds(pl.multiple_of((first + t) * 32 + g, 8), 8), :] for t in range(step + taps - 1)]
            for t in range(step):
                acc = rows[0] * x[t]
                for k in range(1, taps):
                    acc = acc + rows[k] * x[t + k]
                f_ref[pl.ds((first + t) * pitch + g, 8), :] = acc
            return 0

        lax.fori_loop(0, spectra // step, filt, 0)

    def mix(tb, _):
        at = pl.multiple_of(tb * 16, 16)
        for half in range(2):
            here = pl.multiple_of(at + 8 * half, 8)
            re = [f_ref[pl.ds(here * pitch + 2 * m, 8, stride=pitch), :] for m in range(16)]
            im = [f_ref[pl.ds(here * pitch + 2 * m + 1, 8, stride=pitch), :] for m in range(16)]
            out = small_transform(re, im)
            for k in range(16):
                r, i = out[k]
                if k:
                    cos, sin = tw_ref[0, k : k + 1, :], tw_ref[1, k : k + 1, :]
                    r, i = r * cos + i * sin, i * cos - r * sin
                g_ref[0, k, pl.ds(here, 8), :] = r
                g_ref[1, k, pl.ds(here, 8), :] = i
        for k in range(16):
            for c in range(2):
                val = g_ref[c, k, pl.ds(at, 16), :]
                hi = val.astype(BF16)
                ahi_ref[k, pl.ds(at, 16), c * 128 : (c + 1) * 128] = hi
                alo_ref[k, pl.ds(at, 16), c * 128 : (c + 1) * 128] = (val - hi.astype(F32)).astype(BF16)
        return 0

    lax.fori_loop(0, spectra // 16, mix, 0)

    def turn(q, _):
        def dot(a, b):
            return lax.dot_general(a, b, (((1,), (1,)), ((), ())), preferred_element_type=F32)

        weight = w_ref[pl.ds(z_ref[0], 1), :]
        dhi, dlo = dhi_ref[...], dlo_ref[...]
        for i in range(4):
            hi, lo = ahi_ref[4 * q + i], alo_ref[4 * q + i]
            out = dot(dhi, hi) + (dot(dhi, lo) + dot(dlo, hi))
            out = out.astype(BF16).astype(F32) * weight
            for c in range(2):
                m_ref[pl.ds(2 * i + c, 128, stride=8), :] = out[128 * c : 128 * (c + 1)]
        o_ref[pl.ds(pl.multiple_of(q * 1024, 1024), 1024), :] = m_ref[...].astype(BF16)
        return 0

    lax.fori_loop(0, 4, turn, 0)


def channelize(voltages, flags, station, spectra, interpret=False):
    lanes = 2048
    frames = voltages.shape[0] // 32
    taps = frames - spectra + 1
    h = np.repeat(filter_rows(taps, lanes).reshape(taps * 16, 128), 2, axis=0)
    tw = twist_rows(16, 128)
    d = inner_matrix(128, 1.0 / math.sqrt(lanes))
    d = d.reshape(4, 4, 4, 2, 2, 256).transpose(4, 0, 2, 3, 1, 5).reshape(256, 256)
    dhi = d.astype(np.float32).astype(jnp.bfloat16)
    dlo = (d - dhi.astype(np.float64)).astype(np.float32).astype(jnp.bfloat16)
    tables = [jnp.asarray(x) for x in (h, tw, dhi, dlo)]
    return pl.pallas_call(
        channelize_kernel,
        out_shape=jax.ShapeDtypeStruct((4096, spectra), BF16),
        scratch_shapes=[
            pltpu.VMEM(voltages.shape, F32),
            pltpu.VMEM((spectra * 36, 128), F32),
            pltpu.VMEM((2, 16, spectra, 128), F32),
            pltpu.VMEM((16, spectra, 256), BF16),
            pltpu.VMEM((16, spectra, 256), BF16),
            pltpu.VMEM((1024, spectra), F32),
        ],
        in_specs=[pl.BlockSpec(memory_space=pltpu.VMEM)] * 6 + [pl.BlockSpec(memory_space=pltpu.SMEM)],
        interpret=interpret,
        name="channelize",
    )(voltages, *tables, flags, station)


def nt(a, b):
    return lax.dot_general(a, b, (((1,), (1,)), ((), ())), preferred_element_type=F32)


def prepare_kernel(tile_ref, sel_ref, inv_ref):
    rows = sel_ref.shape[0]
    tile = tile_ref[...]
    n = tile.shape[1]
    ids = jnp.transpose(tile)[0:8, :]
    ids = jnp.concatenate([ids[:, 4:], ids[:, :4]], axis=1)
    lane = lax.broadcasted_iota(jnp.int32, (8, rows), 1)
    ids = jnp.where((lane & 7) < 4, ids, -1.0)
    down = lax.broadcasted_iota(jnp.int32, (rows, rows), 0)
    pol = (lane >> 7) & 1
    spot = ((lane >> 3) & 15) * 32 + (lane & 3) * 8 + ((lane >> 2) & 1) * 2 + (lane >> 8)
    move = jnp.where(down == spot[0:1], 1.0, 0.0).astype(BF16)
    moved = jnp.dot(ids.astype(BF16), move, preferred_element_type=F32).astype(jnp.int32)
    source_row = 2 * moved + pol
    sel_ref[...] = jnp.where(down == source_row[0:1], 1.0, 0.0).astype(BF16)
    pick = jnp.where((down >> 1) == ids[0:1].astype(jnp.int32), 1.0, 0.0).astype(BF16)
    hi = tile.astype(BF16)
    rest = tile - hi.astype(F32)
    mid = rest.astype(BF16)
    low = (rest - mid.astype(F32)).astype(BF16)
    placed = jnp.dot(pick, jnp.concatenate([hi, mid, low], axis=1), preferred_element_type=F32).astype(BF16)
    hi, mid, low = placed[:, :n], placed[:, n : 2 * n], placed[:, 2 * n :]
    left = jnp.concatenate([hi, hi, mid, mid, hi, low], axis=1)
    right = jnp.concatenate([hi, mid, hi, mid, low, hi], axis=1)
    inv_ref[...] = 1.0 / jnp.maximum(nt(left, right), 1.0)


def prepare(tile, inputs, interpret=False):
    return pl.pallas_call(
        prepare_kernel,
        out_shape=(jax.ShapeDtypeStruct((inputs, inputs), BF16), jax.ShapeDtypeStruct((inputs, inputs), F32)),
        interpret=interpret,
        compiler_params=pltpu.CompilerParams(vmem_limit_bytes=24 << 20),
        name="prepare",
    )(tile)


def correlate_kernel(x_ref, sel_ref, inv_ref, o_ref, s_ref):
    rows = sel_ref.shape[0]

    @pl.when(pl.program_id(0) == 0)
    def _():
        s_ref[...] = x_ref[...].astype(F32)

    n = rows // 2
    half = x_ref.shape[1]
    below = lax.broadcasted_iota(jnp.int32, (n, n), 0) >= lax.broadcasted_iota(jnp.int32, (n, n), 1)
    ready = []
    for u in range(o_ref.shape[0]):
        at = 2 * (pl.program_id(0) * o_ref.shape[0] + u)
        mine = jnp.concatenate([s_ref[pl.ds(at, rows, stride=8), :], s_ref[pl.ds(at + 1, rows, stride=8), :]], axis=1)
        kept = jnp.dot(sel_ref[...], mine.astype(BF16), preferred_element_type=F32)
        turned = jnp.concatenate([-kept[:, half:], kept[:, :half]], axis=1).astype(BF16)
        ready.append((kept.astype(BF16), turned))
    for u, (plain, turned) in enumerate(ready):
        for a in range(2):
            for b in range(2):
                pa = plain[a * n : (a + 1) * n]
                if a > b:
                    out = nt(pa, plain[b * n : (b + 1) * n])
                elif a < b:
                    out = nt(pa, turned[b * n : (b + 1) * n])
                else:
                    out = jnp.where(below, nt(pa, pa), nt(pa, turned[b * n : (b + 1) * n]))
                inv = inv_ref[a * n : (a + 1) * n, b * n : (b + 1) * n]
                o_ref[u, a * n : (a + 1) * n, b * n : (b + 1) * n] = (out * inv).astype(BF16)


def correlate(arrived, sel, inv, interpret=False):
    inputs = sel.shape[0]
    channels = arrived.shape[0] // (2 * inputs)
    arrived, sel, inv = (pltpu.with_memory_space_constraint(x, pltpu.VMEM) for x in (arrived, sel, inv))
    return pl.pallas_call(
        correlate_kernel,
        grid=(channels // 2,),
        in_specs=[pl.BlockSpec(memory_space=pltpu.VMEM)] * 3,
        out_specs=pl.BlockSpec((2, inputs, inputs), lambda i: (i, 0, 0)),
        out_shape=jax.ShapeDtypeStruct((channels, inputs, inputs), BF16),
        scratch_shapes=[pltpu.VMEM(arrived.shape, F32)],
        interpret=interpret,
        compiler_params=pltpu.CompilerParams(vmem_limit_bytes=24 << 20),
        name="correlate",
    )(arrived, sel, inv)


def tile_kernel(flag_ref, row_ref, o_ref):
    own, n = flag_ref.shape
    down = lax.broadcasted_iota(jnp.int32, (own, n), 0)
    ids = jnp.zeros((own, n), jnp.int32)
    for q in range(own):
        ids = jnp.where(down == q, row_ref[q], ids)
    block = jnp.concatenate([flag_ref[...], ids.astype(F32)], axis=0)
    for d in range(o_ref.shape[0]):
        o_ref[d] = block


def make_tiles(flags, station_row, copies, interpret=False):
    return pl.pallas_call(
        tile_kernel,
        out_shape=jax.ShapeDtypeStruct((copies, 2 * flags.shape[0], flags.shape[1]), F32),
        in_specs=[pl.BlockSpec(memory_space=pltpu.VMEM), pl.BlockSpec(memory_space=pltpu.SMEM)],
        interpret=interpret,
        name="make_tiles",
    )(flags, station_row)


def on_device(voltages, flags, station_row):
    spectra = flags.shape[1]
    z_hi = (2 * lax.axis_index("a") + lax.axis_index("b")).astype(jnp.int32).reshape(1)
    tile = make_tiles(flags, station_row, 64)
    tile = lax.all_to_all(tile, ("x", "y", "l"), split_axis=0, concat_axis=0, tiled=True)
    frames = jnp.transpose(voltages[0].reshape(2, -1, 16, 128), (1, 2, 0, 3)).reshape(-1, 128)
    blocks = channelize(frames, flags, z_hi, spectra).reshape(512, 8, spectra)
    moved = lax.all_to_all(blocks, ("b", "c", "x", "y", "a", "l"), split_axis=0, concat_axis=0, tiled=True)
    sel, inv = prepare(tile.reshape(512, spectra), 512)
    return correlate(moved.reshape(4096, spectra), sel, inv)


def solution(mesh):
    axes = ("x", "l", "y", "a", "b", "c")
    fine = jax.sharding.Mesh(mesh.devices.reshape(4, 4, 4, 2, 2, 2), axes)
    stn = axes[:3]
    return jax.shard_map(
        on_device,
        mesh=fine,
        in_specs=(P(axes, None, None, None), P(stn, None), P(stn)),
        out_specs=P(axes, None, None),
        check_vma=False,
    )
```

```python
import math
import numpy as np
import jax
import jax.numpy as jnp
from jax import lax
from jax.experimental import pallas as pl
from jax.experimental.pallas import tpu as pltpu
from jax.sharding import PartitionSpec as P

F32 = jnp.float32
BF16 = jnp.bfloat16


def filter_rows(taps, lanes):
    total = taps * lanes
    places = np.arange(total, dtype=np.float64) + 0.5
    window = 0.5 - 0.5 * np.cos(2.0 * np.pi * places / total)
    table = np.sinc((places - 0.5 * total) / lanes) * window
    return table.reshape(taps, lanes).astype(np.float32)


def twist_rows(outer, inner):
    k = np.arange(outer)[:, None] * np.arange(inner)[None, :]
    angle = 2.0 * np.pi * k / (outer * inner)
    return np.stack([np.cos(angle), np.sin(angle)]).astype(np.float32)


def inner_matrix(inner, scale):
    jn = np.arange(inner)[:, None] * np.arange(inner)[None, :] % inner
    angle = 2.0 * np.pi * jn / inner
    cos, sin = np.cos(angle) * scale, np.sin(angle) * scale
    real = np.concatenate([cos, sin], axis=1)
    imag = np.concatenate([-sin, cos], axis=1)
    return np.stack([real, imag], axis=1).reshape(2 * inner, 2 * inner)


def small_transform(re, im):
    def four(a, b, c, d):
        (ar, ai), (br, bi), (cr, ci), (dr, di) = a, b, c, d
        pr, pi, qr, qi = ar + cr, ai + ci, ar - cr, ai - ci
        rr, ri, sr, si = br + dr, bi + di, br - dr, bi - di
        return [
            (pr + rr, pi + ri),
            (qr + si, qi - sr),
            (pr - rr, pi - ri),
            (qr - si, qi + sr),
        ]

    x = list(zip(re, im))
    mid = [four(x[b], x[4 + b], x[8 + b], x[12 + b]) for b in range(4)]
    out = [None] * 16
    for p in range(4):
        row = []
        for b in range(4):
            r, i = mid[b][p]
            e = (b * p) % 16
            if e == 0:
                row.append((r, i))
            elif e == 4:
                row.append((i, -r))
            elif e == 2:
                s = math.sqrt(0.5)
                row.append(((r + i) * s, (i - r) * s))
            elif e == 6:
                s = math.sqrt(0.5)
                row.append(((i - r) * s, -(r + i) * s))
            else:
                c, s = math.cos(2 * math.pi * e / 16), math.sin(2 * math.pi * e / 16)
                row.append((r * c + i * s, i * c - r * s))
        done = four(*row)
        for q in range(4):
            out[p + 4 * q] = done[q]
    return out


def channelize_kernel(v_ref, h_ref, tw_ref, dhi_ref, dlo_ref, w_ref, z_ref, o_ref, x_ref, f_ref, g_ref, ahi_ref, alo_ref, m_ref):
    taps = h_ref.shape[0] // 32
    spectra = w_ref.shape[1]

    def widen(f, _):
        at = pl.multiple_of(f * 352, 352)
        x_ref[pl.ds(at, 352), :] = v_ref[pl.ds(at, 352), :].astype(F32)
        return 0

    lax.fori_loop(0, x_ref.shape[0] // 352, widen, 0)
    pitch = f_ref.shape[0] // spectra
    step = 16

    for g in range(0, 32, 8):

        def filt(tb, _):
            first = tb * step
            rows = [h_ref[32 * k + g : 32 * k + g + 8, :] for k in range(taps)]
            x = [x_ref[pl.ds(pl.multiple_of((first + t) * 32 + g, 8), 8), :] for t in range(step + taps - 1)]
            for t in range(step):
                acc = rows[0] * x[t]
                for k in range(1, taps):
                    acc = acc + rows[k] * x[t + k]
                f_ref[pl.ds((first + t) * pitch + g, 8), :] = acc
            return 0

        lax.fori_loop(0, spectra // step, filt, 0)

    def mix(tb, _):
        at = pl.multiple_of(tb * 16, 16)
        for half in range(2):
            here = pl.multiple_of(at + 8 * half, 8)
            re = [f_ref[pl.ds(here * pitch + 2 * m, 8, stride=pitch), :] for m in range(16)]
            im = [f_ref[pl.ds(here * pitch + 2 * m + 1, 8, stride=pitch), :] for m in range(16)]
            out = small_transform(re, im)
            for k in range(16):
                r, i = out[k]
                if k:
                    cos, sin = tw_ref[0, k : k + 1, :], tw_ref[1, k : k + 1, :]
                    r, i = r * cos + i * sin, i * cos - r * sin
                g_ref[0, k, pl.ds(here, 8), :] = r
                g_ref[1, k, pl.ds(here, 8), :] = i
        for k in range(16):
            for c in range(2):
                val = g_ref[c, k, pl.ds(at, 16), :]
                hi = val.astype(BF16)
                ahi_ref[k, pl.ds(at, 16), c * 128 : (c + 1) * 128] = hi
                alo_ref[k, pl.ds(at, 16), c * 128 : (c + 1) * 128] = (val - hi.astype(F32)).astype(BF16)
        return 0

    lax.fori_loop(0, spectra // 16, mix, 0)

    def turn(q, _):
        def dot(a, b):
            return lax.dot_general(a, b, (((1,), (1,)), ((), ())), preferred_element_type=F32)

        weight = w_ref[pl.ds(z_ref[0], 1), :]
        dhi, dlo = dhi_ref[...], dlo_ref[...]
        for i in range(4):
            hi, lo = ahi_ref[4 * q + i], alo_ref[4 * q + i]
            out = dot(dhi, hi) + (dot(dhi, lo) + dot(dlo, hi))
            out = out.astype(BF16).astype(F32) * weight
            for c in range(2):
                m_ref[pl.ds(2 * i + c, 128, stride=8), :] = out[128 * c : 128 * (c + 1)]
        o_ref[pl.ds(pl.multiple_of(q * 1024, 1024), 1024), :] = m_ref[...].astype(BF16)
        return 0

    lax.fori_loop(0, 4, turn, 0)


def channelize(voltages, flags, station, spectra, interpret=False):
    lanes = 2048
    frames = voltages.shape[0] // 32
    taps = frames - spectra + 1
    h = np.repeat(filter_rows(taps, lanes).reshape(taps * 16, 128), 2, axis=0)
    tw = twist_rows(16, 128)
    d = inner_matrix(128, 1.0 / math.sqrt(lanes))
    d = d.reshape(4, 4, 4, 2, 2, 256).transpose(4, 0, 2, 3, 1, 5).reshape(256, 256)
    dhi = d.astype(np.float32).astype(jnp.bfloat16)
    dlo = (d - dhi.astype(np.float64)).astype(np.float32).astype(jnp.bfloat16)
    tables = [jnp.asarray(x) for x in (h, tw, dhi, dlo)]
    return pl.pallas_call(
        channelize_kernel,
        out_shape=jax.ShapeDtypeStruct((4096, spectra), BF16),
        scratch_shapes=[
            pltpu.VMEM(voltages.shape, F32),
            pltpu.VMEM((spectra * 36, 128), F32),
            pltpu.VMEM((2, 16, spectra, 128), F32),
            pltpu.VMEM((16, spectra, 256), BF16),
            pltpu.VMEM((16, spectra, 256), BF16),
            pltpu.VMEM((1024, spectra), F32),
        ],
        in_specs=[pl.BlockSpec(memory_space=pltpu.VMEM)] * 6 + [pl.BlockSpec(memory_space=pltpu.SMEM)],
        interpret=interpret,
        name="channelize",
    )(voltages, *tables, flags, station)


def nt(a, b):
    return lax.dot_general(a, b, (((1,), (1,)), ((), ())), preferred_element_type=F32)


def prepare_kernel(tile_ref, place_ref, sel_ref, inv_ref):
    rows = sel_ref.shape[0]
    tile = tile_ref[...]
    n = tile.shape[1]
    ids = jnp.transpose(tile)[0:8, :]
    ids = jnp.concatenate([ids[:, 4:], ids[:, :4]], axis=1)
    lane = lax.broadcasted_iota(jnp.int32, (8, rows), 1)
    ids = jnp.where((lane & 7) < 4, ids, -1.0)
    down = lax.broadcasted_iota(jnp.int32, (rows, rows), 0)
    pol = (lane >> 7) & 1
    x = (place_ref[0] - ((lane >> 5) & 3)) & 3
    y = (place_ref[1] - ((lane >> 3) & 3)) & 3
    z = (place_ref[2] - (lane & 3)) & 3
    spot = y * 128 + x * 32 + z * 8 + ((lane >> 2) & 1) * 2 + (lane >> 8)
    move = jnp.where(down == spot[0:1], 1.0, 0.0).astype(BF16)
    moved = jnp.dot(ids.astype(BF16), move, preferred_element_type=F32).astype(jnp.int32)
    source_row = 2 * moved + pol
    sel_ref[...] = jnp.where(down == source_row[0:1], 1.0, 0.0).astype(BF16)
    pick = jnp.where((down >> 1) == ids[0:1].astype(jnp.int32), 1.0, 0.0).astype(BF16)
    hi = tile.astype(BF16)
    rest = tile - hi.astype(F32)
    mid = rest.astype(BF16)
    low = (rest - mid.astype(F32)).astype(BF16)
    placed = jnp.dot(pick, jnp.concatenate([hi, mid, low], axis=1), preferred_element_type=F32).astype(BF16)
    hi, mid, low = placed[:, :n], placed[:, n : 2 * n], placed[:, 2 * n :]
    left = jnp.concatenate([hi, hi, mid, mid, hi, low], axis=1)
    right = jnp.concatenate([hi, mid, hi, mid, low, hi], axis=1)
    inv_ref[...] = 1.0 / jnp.maximum(nt(left, right), 1.0)


def prepare(tile, place, inputs, interpret=False):
    return pl.pallas_call(
        prepare_kernel,
        out_shape=(jax.ShapeDtypeStruct((inputs, inputs), BF16), jax.ShapeDtypeStruct((inputs, inputs), F32)),
        interpret=interpret,
        compiler_params=pltpu.CompilerParams(vmem_limit_bytes=24 << 20),
        in_specs=[pl.BlockSpec(memory_space=pltpu.VMEM), pl.BlockSpec(memory_space=pltpu.SMEM)],
        name="prepare",
    )(tile, place)


def correlate_kernel(x_ref, sel_ref, inv_ref, o_ref, s_ref):
    rows = sel_ref.shape[0]

    @pl.when(pl.program_id(0) == 0)
    def _():
        s_ref[...] = x_ref[...].astype(F32)

    n = rows // 2
    half = x_ref.shape[1]
    below = lax.broadcasted_iota(jnp.int32, (n, n), 0) >= lax.broadcasted_iota(jnp.int32, (n, n), 1)
    ready = []
    for u in range(o_ref.shape[0]):
        at = 2 * (pl.program_id(0) * o_ref.shape[0] + u)
        mine = jnp.concatenate([s_ref[pl.ds(at, rows, stride=8), :], s_ref[pl.ds(at + 1, rows, stride=8), :]], axis=1)
        kept = jnp.dot(sel_ref[...], mine.astype(BF16), preferred_element_type=F32)
        turned = jnp.concatenate([-kept[:, half:], kept[:, :half]], axis=1).astype(BF16)
        ready.append((kept.astype(BF16), turned))
    for u, (plain, turned) in enumerate(ready):
        for a in range(2):
            for b in range(2):
                pa = plain[a * n : (a + 1) * n]
                if a > b:
                    out = nt(pa, plain[b * n : (b + 1) * n])
                elif a < b:
                    out = nt(pa, turned[b * n : (b + 1) * n])
                else:
                    out = jnp.where(below, nt(pa, pa), nt(pa, turned[b * n : (b + 1) * n]))
                inv = inv_ref[a * n : (a + 1) * n, b * n : (b + 1) * n]
                o_ref[u, a * n : (a + 1) * n, b * n : (b + 1) * n] = (out * inv).astype(BF16)


def correlate(arrived, sel, inv, interpret=False):
    inputs = sel.shape[0]
    channels = arrived.shape[0] // (2 * inputs)
    arrived, sel, inv = (pltpu.with_memory_space_constraint(x, pltpu.VMEM) for x in (arrived, sel, inv))
    return pl.pallas_call(
        correlate_kernel,
        grid=(channels // 2,),
        in_specs=[pl.BlockSpec(memory_space=pltpu.VMEM)] * 3,
        out_specs=pl.BlockSpec((2, inputs, inputs), lambda i: (i, 0, 0)),
        out_shape=jax.ShapeDtypeStruct((channels, inputs, inputs), BF16),
        scratch_shapes=[pltpu.VMEM(arrived.shape, F32)],
        interpret=interpret,
        compiler_params=pltpu.CompilerParams(vmem_limit_bytes=24 << 20),
        name="correlate",
    )(arrived, sel, inv)


def tile_kernel(flag_ref, row_ref, o_ref):
    own, n = flag_ref.shape
    down = lax.broadcasted_iota(jnp.int32, (own, n), 0)
    ids = jnp.zeros((own, n), jnp.int32)
    for q in range(own):
        ids = jnp.where(down == q, row_ref[q], ids)
    block = jnp.concatenate([flag_ref[...], ids.astype(F32)], axis=0)
    o_ref[...] = block


def make_tile(flags, station_row, interpret=False):
    return pl.pallas_call(
        tile_kernel,
        out_shape=jax.ShapeDtypeStruct((2 * flags.shape[0], flags.shape[1]), F32),
        in_specs=[pl.BlockSpec(memory_space=pltpu.VMEM), pl.BlockSpec(memory_space=pltpu.SMEM)],
        interpret=interpret,
        name="make_tile",
    )(flags, station_row)


def gather_line(tile, axis):
    parts = [tile]
    for shift in range(1, 4):
        parts.append(lax.ppermute(tile, axis, [(i, (i + shift) % 4) for i in range(4)]))
    return jnp.concatenate(parts, axis=0)


def on_device(voltages, flags, station_row):
    spectra = flags.shape[1]
    z_hi = (2 * lax.axis_index("a") + lax.axis_index("b")).astype(jnp.int32).reshape(1)
    frames = jnp.transpose(voltages[0].reshape(2, -1, 16, 128), (1, 2, 0, 3)).reshape(-1, 128)
    tile = make_tile(flags, station_row)
    blocks = channelize(frames, flags, z_hi, spectra).reshape(512, 8, spectra)
    tile, blocks = lax.optimization_barrier((tile, blocks))
    moved = lax.all_to_all(blocks, ("b", "c", "x", "y", "a", "l"), split_axis=0, concat_axis=0, tiled=True)
    for axis in ("l", "x", "y"):
        tile = gather_line(tile, axis)
    place = jnp.stack([lax.axis_index(axis) for axis in ("x", "y", "l")]).astype(jnp.int32)
    sel, inv = prepare(tile, place, 512)
    return correlate(moved.reshape(4096, spectra), sel, inv)


def solution(mesh):
    axes = ("x", "l", "y", "a", "b", "c")
    fine = jax.sharding.Mesh(mesh.devices.reshape(4, 4, 4, 2, 2, 2), axes)
    stn = axes[:3]
    return jax.shard_map(
        on_device,
        mesh=fine,
        in_specs=(P(axes, None, None, None), P(stn, None), P(stn)),
        out_specs=P(axes, None, None),
        check_vma=False,
    )
```

```python
import math
import numpy as np
import jax
import jax.numpy as jnp
from jax import lax
from jax.experimental import pallas as pl
from jax.experimental.pallas import tpu as pltpu
from jax.sharding import PartitionSpec as P

F32 = jnp.float32
BF16 = jnp.bfloat16


def filter_rows(taps, lanes):
    total = taps * lanes
    places = np.arange(total, dtype=np.float64) + 0.5
    window = 0.5 - 0.5 * np.cos(2.0 * np.pi * places / total)
    table = np.sinc((places - 0.5 * total) / lanes) * window
    return table.reshape(taps, lanes).astype(np.float32)


def twist_rows(outer, inner):
    k = np.arange(outer)[:, None] * np.arange(inner)[None, :]
    angle = 2.0 * np.pi * k / (outer * inner)
    return np.stack([np.cos(angle), np.sin(angle)]).astype(np.float32)


def inner_matrix(inner, scale):
    jn = np.arange(inner)[:, None] * np.arange(inner)[None, :] % inner
    angle = 2.0 * np.pi * jn / inner
    cos, sin = np.cos(angle) * scale, np.sin(angle) * scale
    real = np.concatenate([cos, sin], axis=1)
    imag = np.concatenate([-sin, cos], axis=1)
    return np.stack([real, imag], axis=1).reshape(2 * inner, 2 * inner)


def small_transform(re, im):
    def four(a, b, c, d):
        (ar, ai), (br, bi), (cr, ci), (dr, di) = a, b, c, d
        pr, pi, qr, qi = ar + cr, ai + ci, ar - cr, ai - ci
        rr, ri, sr, si = br + dr, bi + di, br - dr, bi - di
        return [
            (pr + rr, pi + ri),
            (qr + si, qi - sr),
            (pr - rr, pi - ri),
            (qr - si, qi + sr),
        ]

    x = list(zip(re, im))
    mid = [four(x[b], x[4 + b], x[8 + b], x[12 + b]) for b in range(4)]
    out = [None] * 16
    for p in range(4):
        row = []
        for b in range(4):
            r, i = mid[b][p]
            e = (b * p) % 16
            if e == 0:
                row.append((r, i))
            elif e == 4:
                row.append((i, -r))
            elif e == 2:
                s = math.sqrt(0.5)
                row.append(((r + i) * s, (i - r) * s))
            elif e == 6:
                s = math.sqrt(0.5)
                row.append(((i - r) * s, -(r + i) * s))
            else:
                c, s = math.cos(2 * math.pi * e / 16), math.sin(2 * math.pi * e / 16)
                row.append((r * c + i * s, i * c - r * s))
        done = four(*row)
        for q in range(4):
            out[p + 4 * q] = done[q]
    return out


def channelize_kernel(v_ref, h_ref, tw_ref, dhi_ref, dlo_ref, w_ref, z_ref, o_ref, x_ref, f_ref, g_ref, ahi_ref, alo_ref, m_ref):
    taps = h_ref.shape[0] // 32
    spectra = w_ref.shape[1]

    def widen(f, _):
        at = pl.multiple_of(f * 352, 352)
        x_ref[pl.ds(at, 352), :] = v_ref[pl.ds(at, 352), :].astype(F32)
        return 0

    lax.fori_loop(0, x_ref.shape[0] // 352, widen, 0)
    pitch = f_ref.shape[0] // spectra
    step = 16

    for g in range(0, 32, 8):

        def filt(tb, _):
            first = tb * step
            rows = [h_ref[32 * k + g : 32 * k + g + 8, :] for k in range(taps)]
            x = [x_ref[pl.ds(pl.multiple_of((first + t) * 32 + g, 8), 8), :] for t in range(step + taps - 1)]
            for t in range(step):
                acc = rows[0] * x[t]
                for k in range(1, taps):
                    acc = acc + rows[k] * x[t + k]
                f_ref[pl.ds((first + t) * pitch + g, 8), :] = acc
            return 0

        lax.fori_loop(0, spectra // step, filt, 0)

    def mix(tb, _):
        at = pl.multiple_of(tb * 16, 16)
        for half in range(2):
            here = pl.multiple_of(at + 8 * half, 8)
            re = [f_ref[pl.ds(here * pitch + 2 * m, 8, stride=pitch), :] for m in range(16)]
            im = [f_ref[pl.ds(here * pitch + 2 * m + 1, 8, stride=pitch), :] for m in range(16)]
            out = small_transform(re, im)
            for k in range(16):
                r, i = out[k]
                if k:
                    cos, sin = tw_ref[0, k : k + 1, :], tw_ref[1, k : k + 1, :]
                    r, i = r * cos + i * sin, i * cos - r * sin
                g_ref[0, k, pl.ds(here, 8), :] = r
                g_ref[1, k, pl.ds(here, 8), :] = i
        for k in range(16):
            for c in range(2):
                val = g_ref[c, k, pl.ds(at, 16), :]
                hi = val.astype(BF16)
                ahi_ref[k, pl.ds(at, 16), c * 128 : (c + 1) * 128] = hi
                alo_ref[k, pl.ds(at, 16), c * 128 : (c + 1) * 128] = (val - hi.astype(F32)).astype(BF16)
        return 0

    lax.fori_loop(0, spectra // 16, mix, 0)

    def turn(q, _):
        def dot(a, b):
            return lax.dot_general(a, b, (((1,), (1,)), ((), ())), preferred_element_type=F32)

        weight = w_ref[pl.ds(z_ref[0], 1), :]
        dhi, dlo = dhi_ref[...], dlo_ref[...]
        for i in range(4):
            hi, lo = ahi_ref[4 * q + i], alo_ref[4 * q + i]
            out = dot(dhi, hi) + (dot(dhi, lo) + dot(dlo, hi))
            out = out.astype(BF16).astype(F32) * weight
            for c in range(2):
                m_ref[pl.ds(2 * i + c, 128, stride=8), :] = out[128 * c : 128 * (c + 1)]
        o_ref[pl.ds(pl.multiple_of(q * 1024, 1024), 1024), :] = m_ref[...].astype(BF16)
        return 0

    lax.fori_loop(0, 4, turn, 0)


def channelize(voltages, flags, station, spectra, interpret=False):
    lanes = 2048
    frames = voltages.shape[0] // 32
    taps = frames - spectra + 1
    h = np.repeat(filter_rows(taps, lanes).reshape(taps * 16, 128), 2, axis=0)
    tw = twist_rows(16, 128)
    d = inner_matrix(128, 1.0 / math.sqrt(lanes))
    d = d.reshape(4, 4, 4, 2, 2, 256).transpose(4, 0, 2, 3, 1, 5).reshape(256, 256)
    dhi = d.astype(np.float32).astype(jnp.bfloat16)
    dlo = (d - dhi.astype(np.float64)).astype(np.float32).astype(jnp.bfloat16)
    tables = [jnp.asarray(x) for x in (h, tw, dhi, dlo)]
    return pl.pallas_call(
        channelize_kernel,
        out_shape=jax.ShapeDtypeStruct((4096, spectra), BF16),
        scratch_shapes=[
            pltpu.VMEM(voltages.shape, F32),
            pltpu.VMEM((spectra * 36, 128), F32),
            pltpu.VMEM((2, 16, spectra, 128), F32),
            pltpu.VMEM((16, spectra, 256), BF16),
            pltpu.VMEM((16, spectra, 256), BF16),
            pltpu.VMEM((1024, spectra), F32),
        ],
        in_specs=[pl.BlockSpec(memory_space=pltpu.VMEM)] * 6 + [pl.BlockSpec(memory_space=pltpu.SMEM)],
        interpret=interpret,
        name="channelize",
    )(voltages, *tables, flags, station)


def nt(a, b):
    return lax.dot_general(a, b, (((1,), (1,)), ((), ())), preferred_element_type=F32)


def prepare_kernel(tile_ref, place_ref, sel_ref, inv_ref):
    rows = sel_ref.shape[0]
    tile = tile_ref[...]
    n = tile.shape[1]
    ids = jnp.transpose(tile)[0:8, :]
    ids = jnp.concatenate([ids[:, 4:], ids[:, :4]], axis=1)
    lane = lax.broadcasted_iota(jnp.int32, (8, rows), 1)
    ids = jnp.where((lane & 7) < 4, ids, -1.0)
    down = lax.broadcasted_iota(jnp.int32, (rows, rows), 0)
    pol = (lane >> 7) & 1
    x = (place_ref[0] - ((lane >> 5) & 3)) & 3
    y = (place_ref[1] - ((lane >> 3) & 3)) & 3
    z = lane & 3
    spot = y * 128 + x * 32 + z * 8 + ((lane >> 2) & 1) * 2 + (lane >> 8)
    move = jnp.where(down == spot[0:1], 1.0, 0.0).astype(BF16)
    moved = jnp.dot(ids.astype(BF16), move, preferred_element_type=F32).astype(jnp.int32)
    source_row = 2 * moved + pol
    sel_ref[...] = jnp.where(down == source_row[0:1], 1.0, 0.0).astype(BF16)
    pick = jnp.where((down >> 1) == ids[0:1].astype(jnp.int32), 1.0, 0.0).astype(BF16)
    hi = tile.astype(BF16)
    rest = tile - hi.astype(F32)
    mid = rest.astype(BF16)
    low = (rest - mid.astype(F32)).astype(BF16)
    placed = jnp.dot(pick, jnp.concatenate([hi, mid, low], axis=1), preferred_element_type=F32).astype(BF16)
    hi, mid, low = placed[:, :n], placed[:, n : 2 * n], placed[:, 2 * n :]
    left = jnp.concatenate([hi, hi, mid, mid, hi, low], axis=1)
    right = jnp.concatenate([hi, mid, hi, mid, low, hi], axis=1)
    inv_ref[...] = 1.0 / jnp.maximum(nt(left, right), 1.0)


def prepare(tile, place, inputs, interpret=False):
    return pl.pallas_call(
        prepare_kernel,
        out_shape=(jax.ShapeDtypeStruct((inputs, inputs), BF16), jax.ShapeDtypeStruct((inputs, inputs), F32)),
        interpret=interpret,
        compiler_params=pltpu.CompilerParams(vmem_limit_bytes=24 << 20),
        in_specs=[pl.BlockSpec(memory_space=pltpu.VMEM), pl.BlockSpec(memory_space=pltpu.SMEM)],
        name="prepare",
    )(tile, place)


def correlate_kernel(x_ref, sel_ref, inv_ref, o_ref, s_ref):
    rows = sel_ref.shape[0]

    @pl.when(pl.program_id(0) == 0)
    def _():
        s_ref[...] = x_ref[...].astype(F32)

    n = rows // 2
    half = x_ref.shape[1]
    below = lax.broadcasted_iota(jnp.int32, (n, n), 0) >= lax.broadcasted_iota(jnp.int32, (n, n), 1)
    ready = []
    for u in range(o_ref.shape[0]):
        at = 2 * (pl.program_id(0) * o_ref.shape[0] + u)
        mine = jnp.concatenate([s_ref[pl.ds(at, rows, stride=8), :], s_ref[pl.ds(at + 1, rows, stride=8), :]], axis=1)
        kept = jnp.dot(sel_ref[...], mine.astype(BF16), preferred_element_type=F32)
        turned = jnp.concatenate([-kept[:, half:], kept[:, :half]], axis=1).astype(BF16)
        ready.append((kept.astype(BF16), turned))
    for u, (plain, turned) in enumerate(ready):
        for a in range(2):
            for b in range(2):
                pa = plain[a * n : (a + 1) * n]
                if a > b:
                    out = nt(pa, plain[b * n : (b + 1) * n])
                elif a < b:
                    out = nt(pa, turned[b * n : (b + 1) * n])
                else:
                    out = jnp.where(below, nt(pa, pa), nt(pa, turned[b * n : (b + 1) * n]))
                inv = inv_ref[a * n : (a + 1) * n, b * n : (b + 1) * n]
                o_ref[u, a * n : (a + 1) * n, b * n : (b + 1) * n] = (out * inv).astype(BF16)


def correlate(arrived, sel, inv, interpret=False):
    inputs = sel.shape[0]
    channels = arrived.shape[0] // (2 * inputs)
    arrived, sel, inv = (pltpu.with_memory_space_constraint(x, pltpu.VMEM) for x in (arrived, sel, inv))
    return pl.pallas_call(
        correlate_kernel,
        grid=(channels // 2,),
        in_specs=[pl.BlockSpec(memory_space=pltpu.VMEM)] * 3,
        out_specs=pl.BlockSpec((2, inputs, inputs), lambda i: (i, 0, 0)),
        out_shape=jax.ShapeDtypeStruct((channels, inputs, inputs), BF16),
        scratch_shapes=[pltpu.VMEM(arrived.shape, F32)],
        interpret=interpret,
        compiler_params=pltpu.CompilerParams(vmem_limit_bytes=24 << 20),
        name="correlate",
    )(arrived, sel, inv)


def tile_kernel(flag_ref, row_ref, o_ref):
    own, n = flag_ref.shape
    down = lax.broadcasted_iota(jnp.int32, (own, n), 0)
    ids = jnp.zeros((own, n), jnp.int32)
    for q in range(own):
        ids = jnp.where(down == q, row_ref[q], ids)
    block = jnp.concatenate([flag_ref[...], ids.astype(F32)], axis=0)
    for d in range(o_ref.shape[0]):
        o_ref[d] = block


def make_tiles(flags, station_row, copies, interpret=False):
    return pl.pallas_call(
        tile_kernel,
        out_shape=jax.ShapeDtypeStruct((copies, 2 * flags.shape[0], flags.shape[1]), F32),
        in_specs=[pl.BlockSpec(memory_space=pltpu.VMEM), pl.BlockSpec(memory_space=pltpu.SMEM)],
        interpret=interpret,
        name="make_tiles",
    )(flags, station_row)


def gather_line(tile, axis):
    parts = [tile]
    for shift in range(1, 4):
        parts.append(lax.ppermute(tile, axis, [(i, (i + shift) % 4) for i in range(4)]))
    return jnp.concatenate(parts, axis=0)


def on_device(voltages, flags, station_row):
    spectra = flags.shape[1]
    z_hi = (2 * lax.axis_index("a") + lax.axis_index("b")).astype(jnp.int32).reshape(1)
    frames = jnp.transpose(voltages[0].reshape(2, -1, 16, 128), (1, 2, 0, 3)).reshape(-1, 128)
    tile = make_tiles(flags, station_row, 4)
    tile = lax.all_to_all(tile, "l", split_axis=0, concat_axis=0, tiled=True).reshape(32, spectra)
    blocks = channelize(frames, flags, z_hi, spectra).reshape(512, 8, spectra)
    tile, blocks = lax.optimization_barrier((tile, blocks))
    moved = lax.all_to_all(blocks, ("b", "c", "x", "y", "a", "l"), split_axis=0, concat_axis=0, tiled=True)
    for axis in ("x", "y"):
        tile = gather_line(tile, axis)
    place = jnp.stack([lax.axis_index(axis) for axis in ("x", "y")]).astype(jnp.int32)
    sel, inv = prepare(tile, place, 512)
    return correlate(moved.reshape(4096, spectra), sel, inv)


def solution(mesh):
    axes = ("x", "l", "y", "a", "b", "c")
    fine = jax.sharding.Mesh(mesh.devices.reshape(4, 4, 4, 2, 2, 2), axes)
    stn = axes[:3]
    return jax.shard_map(
        on_device,
        mesh=fine,
        in_specs=(P(axes, None, None, None), P(stn, None), P(stn)),
        out_specs=P(axes, None, None),
        check_vma=False,
    )
```

```python
import math
import numpy as np
import jax
import jax.numpy as jnp
from jax import lax
from jax.experimental import pallas as pl
from jax.experimental.pallas import tpu as pltpu
from jax.sharding import PartitionSpec as P

F32 = jnp.float32
BF16 = jnp.bfloat16


def filter_rows(taps, lanes):
    total = taps * lanes
    places = np.arange(total, dtype=np.float64) + 0.5
    window = 0.5 - 0.5 * np.cos(2.0 * np.pi * places / total)
    table = np.sinc((places - 0.5 * total) / lanes) * window
    return table.reshape(taps, lanes).astype(np.float32)


def twist_rows(outer, inner):
    k = np.arange(outer)[:, None] * np.arange(inner)[None, :]
    angle = 2.0 * np.pi * k / (outer * inner)
    return np.stack([np.cos(angle), np.sin(angle)]).astype(np.float32)


def inner_matrix(inner, scale):
    jn = np.arange(inner)[:, None] * np.arange(inner)[None, :] % inner
    angle = 2.0 * np.pi * jn / inner
    cos, sin = np.cos(angle) * scale, np.sin(angle) * scale
    real = np.concatenate([cos, sin], axis=1)
    imag = np.concatenate([-sin, cos], axis=1)
    return np.stack([real, imag], axis=1).reshape(2 * inner, 2 * inner)


def small_transform(re, im):
    def four(a, b, c, d):
        (ar, ai), (br, bi), (cr, ci), (dr, di) = a, b, c, d
        pr, pi, qr, qi = ar + cr, ai + ci, ar - cr, ai - ci
        rr, ri, sr, si = br + dr, bi + di, br - dr, bi - di
        return [
            (pr + rr, pi + ri),
            (qr + si, qi - sr),
            (pr - rr, pi - ri),
            (qr - si, qi + sr),
        ]

    x = list(zip(re, im))
    mid = [four(x[b], x[4 + b], x[8 + b], x[12 + b]) for b in range(4)]
    out = [None] * 16
    for p in range(4):
        row = []
        for b in range(4):
            r, i = mid[b][p]
            e = (b * p) % 16
            if e == 0:
                row.append((r, i))
            elif e == 4:
                row.append((i, -r))
            elif e == 2:
                s = math.sqrt(0.5)
                row.append(((r + i) * s, (i - r) * s))
            elif e == 6:
                s = math.sqrt(0.5)
                row.append(((i - r) * s, -(r + i) * s))
            else:
                c, s = math.cos(2 * math.pi * e / 16), math.sin(2 * math.pi * e / 16)
                row.append((r * c + i * s, i * c - r * s))
        done = four(*row)
        for q in range(4):
            out[p + 4 * q] = done[q]
    return out


def channelize_kernel(v_ref, h_ref, tw_ref, dhi_ref, dlo_ref, w_ref, z_ref, o_ref, x_ref, f_ref, g_ref, ahi_ref, alo_ref, m_ref):
    taps = h_ref.shape[0] // 32
    spectra = w_ref.shape[1]

    def widen(f, _):
        at = pl.multiple_of(f * 352, 352)
        x_ref[pl.ds(at, 352), :] = v_ref[pl.ds(at, 352), :].astype(F32)
        return 0

    lax.fori_loop(0, x_ref.shape[0] // 352, widen, 0)
    pitch = f_ref.shape[0] // spectra
    step = 16

    for g in range(0, 32, 8):

        def filt(tb, _):
            first = tb * step
            rows = [h_ref[32 * k + g : 32 * k + g + 8, :] for k in range(taps)]
            x = [x_ref[pl.ds(pl.multiple_of((first + t) * 32 + g, 8), 8), :] for t in range(step + taps - 1)]
            for t in range(step):
                acc = rows[0] * x[t]
                for k in range(1, taps):
                    acc = acc + rows[k] * x[t + k]
                f_ref[pl.ds((first + t) * pitch + g, 8), :] = acc
            return 0

        lax.fori_loop(0, spectra // step, filt, 0)

    def mix(tb, _):
        at = pl.multiple_of(tb * 16, 16)
        for half in range(2):
            here = pl.multiple_of(at + 8 * half, 8)
            re = [f_ref[pl.ds(here * pitch + 2 * m, 8, stride=pitch), :] for m in range(16)]
            im = [f_ref[pl.ds(here * pitch + 2 * m + 1, 8, stride=pitch), :] for m in range(16)]
            out = small_transform(re, im)
            for k in range(16):
                r, i = out[k]
                if k:
                    cos, sin = tw_ref[0, k : k + 1, :], tw_ref[1, k : k + 1, :]
                    r, i = r * cos + i * sin, i * cos - r * sin
                g_ref[0, k, pl.ds(here, 8), :] = r
                g_ref[1, k, pl.ds(here, 8), :] = i
        for k in range(16):
            for c in range(2):
                val = g_ref[c, k, pl.ds(at, 16), :]
                hi = val.astype(BF16)
                ahi_ref[k, pl.ds(at, 16), c * 128 : (c + 1) * 128] = hi
                alo_ref[k, pl.ds(at, 16), c * 128 : (c + 1) * 128] = (val - hi.astype(F32)).astype(BF16)
        return 0

    lax.fori_loop(0, spectra // 16, mix, 0)

    def dot(a, b):
        return lax.dot_general(a, b, (((1,), (1,)), ((), ())), preferred_element_type=F32)

    weight = w_ref[pl.ds(z_ref[0], 1), :]
    dhi, dlo = dhi_ref[...], dlo_ref[...]
    for q in range(4):
        for i in range(4):
            hi = ahi_ref[4 * q + i]
            out = dot(dhi, hi) + (dot(dhi, alo_ref[4 * q + i]) + dot(dlo, hi))
            out = out.astype(BF16).astype(F32) * weight
            for c in range(2):
                m_ref[pl.ds(1024 * q + 2 * i + c, 128, stride=8), :] = out[128 * c : 128 * (c + 1)]
        o_ref[1024 * q : 1024 * (q + 1), :] = m_ref[1024 * q : 1024 * (q + 1), :].astype(BF16)


def channelize(voltages, flags, station, spectra, interpret=False):
    lanes = 2048
    frames = voltages.shape[0] // 32
    taps = frames - spectra + 1
    h = np.repeat(filter_rows(taps, lanes).reshape(taps * 16, 128), 2, axis=0)
    tw = twist_rows(16, 128)
    d = inner_matrix(128, 1.0 / math.sqrt(lanes))
    d = d.reshape(4, 4, 4, 2, 2, 256).transpose(4, 0, 2, 3, 1, 5).reshape(256, 256)
    dhi = d.astype(np.float32).astype(jnp.bfloat16)
    dlo = (d - dhi.astype(np.float64)).astype(np.float32).astype(jnp.bfloat16)
    tables = [jnp.asarray(x) for x in (h, tw, dhi, dlo)]
    return pl.pallas_call(
        channelize_kernel,
        out_shape=jax.ShapeDtypeStruct((4096, spectra), BF16),
        scratch_shapes=[
            pltpu.VMEM(voltages.shape, F32),
            pltpu.VMEM((spectra * 36, 128), F32),
            pltpu.VMEM((2, 16, spectra, 128), F32),
            pltpu.VMEM((16, spectra, 256), BF16),
            pltpu.VMEM((16, spectra, 256), BF16),
            pltpu.VMEM((4096, spectra), F32),
        ],
        in_specs=[pl.BlockSpec(memory_space=pltpu.VMEM)] * 6 + [pl.BlockSpec(memory_space=pltpu.SMEM)],
        interpret=interpret,
        name="channelize",
    )(voltages, *tables, flags, station)


def nt(a, b):
    return lax.dot_general(a, b, (((1,), (1,)), ((), ())), preferred_element_type=F32)


def prepare_kernel(tile_ref, place_ref, sel_ref, inv_ref):
    rows = sel_ref.shape[0]
    tile = tile_ref[...]
    n = tile.shape[1]
    ids = jnp.transpose(tile)[0:8, :]
    ids = jnp.concatenate([ids[:, 4:], ids[:, :4]], axis=1)
    lane = lax.broadcasted_iota(jnp.int32, (8, rows), 1)
    ids = jnp.where((lane & 7) < 4, ids, -1.0)
    down = lax.broadcasted_iota(jnp.int32, (rows, rows), 0)
    pol = (lane >> 7) & 1
    x = (place_ref[0] - ((lane >> 5) & 3)) & 3
    y = (place_ref[1] - ((lane >> 3) & 3)) & 3
    z = lane & 3
    spot = y * 128 + x * 32 + z * 8 + ((lane >> 2) & 1) * 2 + (lane >> 8)
    move = jnp.where(down == spot[0:1], 1.0, 0.0).astype(BF16)
    moved = jnp.dot(ids.astype(BF16), move, preferred_element_type=F32).astype(jnp.int32)
    source_row = 2 * moved + pol
    sel_ref[...] = jnp.where(down == source_row[0:1], 1.0, 0.0).astype(BF16)
    pick = jnp.where((down >> 1) == ids[0:1].astype(jnp.int32), 1.0, 0.0).astype(BF16)
    hi = tile.astype(BF16)
    rest = tile - hi.astype(F32)
    mid = rest.astype(BF16)
    low = (rest - mid.astype(F32)).astype(BF16)
    placed = jnp.dot(pick, jnp.concatenate([hi, mid, low], axis=1), preferred_element_type=F32).astype(BF16)
    hi, mid, low = placed[:, :n], placed[:, n : 2 * n], placed[:, 2 * n :]
    left = jnp.concatenate([hi, hi, mid, mid, hi, low], axis=1)
    right = jnp.concatenate([hi, mid, hi, mid, low, hi], axis=1)
    inv_ref[...] = 1.0 / jnp.maximum(nt(left, right), 1.0)


def prepare(tile, place, inputs, interpret=False):
    return pl.pallas_call(
        prepare_kernel,
        out_shape=(jax.ShapeDtypeStruct((inputs, inputs), BF16), jax.ShapeDtypeStruct((inputs, inputs), F32)),
        interpret=interpret,
        compiler_params=pltpu.CompilerParams(vmem_limit_bytes=24 << 20),
        in_specs=[pl.BlockSpec(memory_space=pltpu.VMEM), pl.BlockSpec(memory_space=pltpu.SMEM)],
        name="prepare",
    )(tile, place)


def correlate_kernel(x_ref, sel_ref, inv_ref, o_ref, s_ref):
    rows = sel_ref.shape[0]

    @pl.when(pl.program_id(0) == 0)
    def _():
        s_ref[...] = x_ref[...].astype(F32)

    n = rows // 2
    half = x_ref.shape[1]
    below = lax.broadcasted_iota(jnp.int32, (n, n), 0) >= lax.broadcasted_iota(jnp.int32, (n, n), 1)
    ready = []
    for u in range(o_ref.shape[0]):
        at = 2 * (pl.program_id(0) * o_ref.shape[0] + u)
        mine = jnp.concatenate([s_ref[pl.ds(at, rows, stride=8), :], s_ref[pl.ds(at + 1, rows, stride=8), :]], axis=1)
        kept = jnp.dot(sel_ref[...], mine.astype(BF16), preferred_element_type=F32)
        turned = jnp.concatenate([-kept[:, half:], kept[:, :half]], axis=1).astype(BF16)
        ready.append((kept.astype(BF16), turned))
    for u, (plain, turned) in enumerate(ready):
        for a in range(2):
            for b in range(2):
                pa = plain[a * n : (a + 1) * n]
                if a > b:
                    out = nt(pa, plain[b * n : (b + 1) * n])
                elif a < b:
                    out = nt(pa, turned[b * n : (b + 1) * n])
                else:
                    out = jnp.where(below, nt(pa, pa), nt(pa, turned[b * n : (b + 1) * n]))
                inv = inv_ref[a * n : (a + 1) * n, b * n : (b + 1) * n]
                o_ref[u, a * n : (a + 1) * n, b * n : (b + 1) * n] = (out * inv).astype(BF16)


def correlate(arrived, sel, inv, interpret=False):
    inputs = sel.shape[0]
    channels = arrived.shape[0] // (2 * inputs)
    arrived, sel, inv = (pltpu.with_memory_space_constraint(x, pltpu.VMEM) for x in (arrived, sel, inv))
    return pl.pallas_call(
        correlate_kernel,
        grid=(channels // 2,),
        in_specs=[pl.BlockSpec(memory_space=pltpu.VMEM)] * 3,
        out_specs=pl.BlockSpec((2, inputs, inputs), lambda i: (i, 0, 0)),
        out_shape=jax.ShapeDtypeStruct((channels, inputs, inputs), BF16),
        scratch_shapes=[pltpu.VMEM(arrived.shape, F32)],
        interpret=interpret,
        compiler_params=pltpu.CompilerParams(vmem_limit_bytes=24 << 20),
        name="correlate",
    )(arrived, sel, inv)


def tile_kernel(flag_ref, row_ref, o_ref):
    own, n = flag_ref.shape
    down = lax.broadcasted_iota(jnp.int32, (own, n), 0)
    ids = jnp.zeros((own, n), jnp.int32)
    for q in range(own):
        ids = jnp.where(down == q, row_ref[q], ids)
    block = jnp.concatenate([flag_ref[...], ids.astype(F32)], axis=0)
    for d in range(o_ref.shape[0]):
        o_ref[d] = block


def make_tiles(flags, station_row, copies, interpret=False):
    return pl.pallas_call(
        tile_kernel,
        out_shape=jax.ShapeDtypeStruct((copies, 2 * flags.shape[0], flags.shape[1]), F32),
        in_specs=[pl.BlockSpec(memory_space=pltpu.VMEM), pl.BlockSpec(memory_space=pltpu.SMEM)],
        interpret=interpret,
        name="make_tiles",
    )(flags, station_row)


def gather_line(tile, axis):
    parts = [tile]
    for shift in range(1, 4):
        parts.append(lax.ppermute(tile, axis, [(i, (i + shift) % 4) for i in range(4)]))
    return jnp.concatenate(parts, axis=0)


def on_device(voltages, flags, station_row):
    spectra = flags.shape[1]
    z_hi = (2 * lax.axis_index("a") + lax.axis_index("b")).astype(jnp.int32).reshape(1)
    frames = jnp.transpose(voltages[0].reshape(2, -1, 16, 128), (1, 2, 0, 3)).reshape(-1, 128)
    tile = make_tiles(flags, station_row, 4)
    tile = lax.all_to_all(tile, "l", split_axis=0, concat_axis=0, tiled=True).reshape(32, spectra)
    blocks = channelize(frames, flags, z_hi, spectra).reshape(512, 8, spectra)
    tile, blocks = lax.optimization_barrier((tile, blocks))
    moved = lax.all_to_all(blocks, ("b", "c", "x", "y", "a", "l"), split_axis=0, concat_axis=0, tiled=True)
    for axis in ("x", "y"):
        tile = gather_line(tile, axis)
    place = jnp.stack([lax.axis_index(axis) for axis in ("x", "y")]).astype(jnp.int32)
    sel, inv = prepare(tile, place, 512)
    return correlate(moved.reshape(4096, spectra), sel, inv)


def solution(mesh):
    axes = ("x", "l", "y", "a", "b", "c")
    fine = jax.sharding.Mesh(mesh.devices.reshape(4, 4, 4, 2, 2, 2), axes)
    stn = axes[:3]
    return jax.shard_map(
        on_device,
        mesh=fine,
        in_specs=(P(axes, None, None, None), P(stn, None), P(stn)),
        out_specs=P(axes, None, None),
        check_vma=False,
    )
```

```python
import math
import numpy as np
import jax
import jax.numpy as jnp
from jax import lax
from jax.experimental import pallas as pl
from jax.experimental.pallas import tpu as pltpu
from jax.sharding import PartitionSpec as P

F32 = jnp.float32
BF16 = jnp.bfloat16


def filter_rows(taps, lanes):
    total = taps * lanes
    places = np.arange(total, dtype=np.float64) + 0.5
    window = 0.5 - 0.5 * np.cos(2.0 * np.pi * places / total)
    table = np.sinc((places - 0.5 * total) / lanes) * window
    return table.reshape(taps, lanes).astype(np.float32)


def twist_rows(outer, inner):
    k = np.arange(outer)[:, None] * np.arange(inner)[None, :]
    angle = 2.0 * np.pi * k / (outer * inner)
    return np.stack([np.cos(angle), np.sin(angle)]).astype(np.float32)


def inner_matrix(inner, scale):
    jn = np.arange(inner)[:, None] * np.arange(inner)[None, :] % inner
    angle = 2.0 * np.pi * jn / inner
    cos, sin = np.cos(angle) * scale, np.sin(angle) * scale
    real = np.concatenate([cos, sin], axis=1)
    imag = np.concatenate([-sin, cos], axis=1)
    return np.stack([real, imag], axis=1).reshape(2 * inner, 2 * inner)


def small_transform(re, im):
    def four(a, b, c, d):
        (ar, ai), (br, bi), (cr, ci), (dr, di) = a, b, c, d
        pr, pi, qr, qi = ar + cr, ai + ci, ar - cr, ai - ci
        rr, ri, sr, si = br + dr, bi + di, br - dr, bi - di
        return [
            (pr + rr, pi + ri),
            (qr + si, qi - sr),
            (pr - rr, pi - ri),
            (qr - si, qi + sr),
        ]

    x = list(zip(re, im))
    mid = [four(x[b], x[4 + b], x[8 + b], x[12 + b]) for b in range(4)]
    out = [None] * 16
    for p in range(4):
        row = []
        for b in range(4):
            r, i = mid[b][p]
            e = (b * p) % 16
            if e == 0:
                row.append((r, i))
            elif e == 4:
                row.append((i, -r))
            elif e == 2:
                s = math.sqrt(0.5)
                row.append(((r + i) * s, (i - r) * s))
            elif e == 6:
                s = math.sqrt(0.5)
                row.append(((i - r) * s, -(r + i) * s))
            else:
                c, s = math.cos(2 * math.pi * e / 16), math.sin(2 * math.pi * e / 16)
                row.append((r * c + i * s, i * c - r * s))
        done = four(*row)
        for q in range(4):
            out[p + 4 * q] = done[q]
    return out


def channelize_kernel(v_ref, h_ref, tw_ref, dhi_ref, dlo_ref, w_ref, z_ref, o_ref, x_ref, f_ref, g_ref, ahi_ref, alo_ref, m_ref):
    taps = h_ref.shape[0] // 32
    spectra = w_ref.shape[1]

    def widen(f, _):
        at = pl.multiple_of(f * 352, 352)
        x_ref[pl.ds(at, 352), :] = v_ref[pl.ds(at, 352), :].astype(F32)
        return 0

    lax.fori_loop(0, x_ref.shape[0] // 352, widen, 0)
    pitch = f_ref.shape[0] // spectra
    step = 16

    for g in range(0, 32, 8):

        def filt(tb, _):
            first = tb * step
            rows = [h_ref[32 * k + g : 32 * k + g + 8, :] for k in range(taps)]
            x = [x_ref[pl.ds(pl.multiple_of((first + t) * 32 + g, 8), 8), :] for t in range(step + taps - 1)]
            for t in range(step):
                acc = rows[0] * x[t]
                for k in range(1, taps):
                    acc = acc + rows[k] * x[t + k]
                f_ref[pl.ds((first + t) * pitch + g, 8), :] = acc
            return 0

        lax.fori_loop(0, spectra // step, filt, 0)

    def mix(tb, _):
        at = pl.multiple_of(tb * 16, 16)
        for half in range(2):
            here = pl.multiple_of(at + 8 * half, 8)
            re = [f_ref[pl.ds(here * pitch + 2 * m, 8, stride=pitch), :] for m in range(16)]
            im = [f_ref[pl.ds(here * pitch + 2 * m + 1, 8, stride=pitch), :] for m in range(16)]
            out = small_transform(re, im)
            for k in range(16):
                r, i = out[k]
                if k:
                    cos, sin = tw_ref[0, k : k + 1, :], tw_ref[1, k : k + 1, :]
                    r, i = r * cos + i * sin, i * cos - r * sin
                g_ref[0, k, pl.ds(here, 8), :] = r
                g_ref[1, k, pl.ds(here, 8), :] = i
        for k in range(16):
            for c in range(2):
                val = g_ref[c, k, pl.ds(at, 16), :]
                hi = val.astype(BF16)
                ahi_ref[k, pl.ds(at, 16), c * 128 : (c + 1) * 128] = hi
                alo_ref[k, pl.ds(at, 16), c * 128 : (c + 1) * 128] = (val - hi.astype(F32)).astype(BF16)
        return 0

    lax.fori_loop(0, spectra // 16, mix, 0)

    def dot(a, b):
        return lax.dot_general(a, b, (((1,), (1,)), ((), ())), preferred_element_type=F32)

    weight = w_ref[pl.ds(z_ref[0], 1), :]
    dhi, dlo = dhi_ref[...], dlo_ref[...]
    for q in range(4):
        starts = [2048 * (q % 2) + 1024 * a + 512 * (q // 2) for a in range(2)]
        for i in range(4):
            hi = ahi_ref[4 * q + i]
            out = dot(dhi, hi) + (dot(dhi, alo_ref[4 * q + i]) + dot(dlo, hi))
            out = out.astype(BF16).astype(F32) * weight
            for c in range(2):
                for a in range(2):
                    rows = out[128 * c + 64 * a : 128 * c + 64 * (a + 1)]
                    m_ref[pl.ds(starts[a] + 2 * i + c, 64, stride=8), :] = rows
        for start in starts:
            o_ref[start : start + 512, :] = m_ref[start : start + 512, :].astype(BF16)


def channelize(voltages, flags, station, spectra, interpret=False):
    lanes = 2048
    frames = voltages.shape[0] // 32
    taps = frames - spectra + 1
    h = np.repeat(filter_rows(taps, lanes).reshape(taps * 16, 128), 2, axis=0)
    tw = twist_rows(16, 128)
    d = inner_matrix(128, 1.0 / math.sqrt(lanes))
    d = d.reshape(4, 4, 4, 2, 2, 256).transpose(4, 3, 1, 0, 2, 5).reshape(256, 256)
    dhi = d.astype(np.float32).astype(jnp.bfloat16)
    dlo = (d - dhi.astype(np.float64)).astype(np.float32).astype(jnp.bfloat16)
    tables = [jnp.asarray(x) for x in (h, tw, dhi, dlo)]
    return pl.pallas_call(
        channelize_kernel,
        out_shape=jax.ShapeDtypeStruct((4096, spectra), BF16),
        scratch_shapes=[
            pltpu.VMEM(voltages.shape, F32),
            pltpu.VMEM((spectra * 36, 128), F32),
            pltpu.VMEM((2, 16, spectra, 128), F32),
            pltpu.VMEM((16, spectra, 256), BF16),
            pltpu.VMEM((16, spectra, 256), BF16),
            pltpu.VMEM((4096, spectra), F32),
        ],
        in_specs=[pl.BlockSpec(memory_space=pltpu.VMEM)] * 6 + [pl.BlockSpec(memory_space=pltpu.SMEM)],
        interpret=interpret,
        name="channelize",
    )(voltages, *tables, flags, station)


def nt(a, b):
    return lax.dot_general(a, b, (((1,), (1,)), ((), ())), preferred_element_type=F32)


def prepare_kernel(tile_ref, place_ref, sel_ref, inv_ref):
    rows = sel_ref.shape[0]
    tile = tile_ref[...]
    n = tile.shape[1]
    ids = jnp.transpose(tile)[0:8, :]
    ids = jnp.concatenate([ids[:, 4:], ids[:, :4]], axis=1)
    lane = lax.broadcasted_iota(jnp.int32, (8, rows), 1)
    ids = jnp.where((lane & 7) < 4, ids, -1.0)
    down = lax.broadcasted_iota(jnp.int32, (rows, rows), 0)
    pol = lane >> 8
    x = (place_ref[0] - ((lane >> 2) & 3)) & 3
    y = (place_ref[1] - (lane & 3)) & 3
    z = (lane >> 4) & 3
    spot = y * 128 + x * 32 + z * 8 + ((lane >> 7) & 1) * 2 + ((lane >> 6) & 1)
    move = jnp.where(down == spot[0:1], 1.0, 0.0).astype(BF16)
    moved = jnp.dot(ids.astype(BF16), move, preferred_element_type=F32).astype(jnp.int32)
    source_row = 2 * moved + pol
    sel_ref[...] = jnp.where(down == source_row[0:1], 1.0, 0.0).astype(BF16)
    pick = jnp.where((down >> 1) == ids[0:1].astype(jnp.int32), 1.0, 0.0).astype(BF16)
    hi = tile.astype(BF16)
    rest = tile - hi.astype(F32)
    mid = rest.astype(BF16)
    low = (rest - mid.astype(F32)).astype(BF16)
    placed = jnp.dot(pick, jnp.concatenate([hi, mid, low], axis=1), preferred_element_type=F32).astype(BF16)
    hi, mid, low = placed[:, :n], placed[:, n : 2 * n], placed[:, 2 * n :]
    left = jnp.concatenate([hi, hi, mid, mid, hi, low], axis=1)
    right = jnp.concatenate([hi, mid, hi, mid, low, hi], axis=1)
    inv_ref[...] = 1.0 / jnp.maximum(nt(left, right), 1.0)


def prepare(tile, place, inputs, interpret=False):
    return pl.pallas_call(
        prepare_kernel,
        out_shape=(jax.ShapeDtypeStruct((inputs, inputs), BF16), jax.ShapeDtypeStruct((inputs, inputs), F32)),
        interpret=interpret,
        compiler_params=pltpu.CompilerParams(vmem_limit_bytes=24 << 20),
        in_specs=[pl.BlockSpec(memory_space=pltpu.VMEM), pl.BlockSpec(memory_space=pltpu.SMEM)],
        name="prepare",
    )(tile, place)


def correlate_kernel(x_ref, sel_ref, inv_ref, o_ref, s_ref):
    rows = sel_ref.shape[0]

    @pl.when(pl.program_id(0) == 0)
    def _():
        s_ref[...] = x_ref[...].astype(F32)

    n = rows // 2
    half = x_ref.shape[1]
    below = lax.broadcasted_iota(jnp.int32, (n, n), 0) >= lax.broadcasted_iota(jnp.int32, (n, n), 1)
    ready = []
    for u in range(o_ref.shape[0]):
        at = 2 * (pl.program_id(0) * o_ref.shape[0] + u)
        mine = jnp.concatenate([s_ref[pl.ds(at, rows, stride=8), :], s_ref[pl.ds(at + 1, rows, stride=8), :]], axis=1)
        kept = jnp.dot(sel_ref[...], mine.astype(BF16), preferred_element_type=F32)
        turned = jnp.concatenate([-kept[:, half:], kept[:, :half]], axis=1).astype(BF16)
        ready.append((kept.astype(BF16), turned))
    for u, (plain, turned) in enumerate(ready):
        for a in range(2):
            for b in range(2):
                pa = plain[a * n : (a + 1) * n]
                if a > b:
                    out = nt(pa, plain[b * n : (b + 1) * n])
                elif a < b:
                    out = nt(pa, turned[b * n : (b + 1) * n])
                else:
                    out = jnp.where(below, nt(pa, pa), nt(pa, turned[b * n : (b + 1) * n]))
                inv = inv_ref[a * n : (a + 1) * n, b * n : (b + 1) * n]
                o_ref[u, a * n : (a + 1) * n, b * n : (b + 1) * n] = (out * inv).astype(BF16)


def correlate(arrived, sel, inv, interpret=False):
    inputs = sel.shape[0]
    channels = arrived.shape[0] // (2 * inputs)
    arrived, sel, inv = (pltpu.with_memory_space_constraint(x, pltpu.VMEM) for x in (arrived, sel, inv))
    return pl.pallas_call(
        correlate_kernel,
        grid=(channels // 2,),
        in_specs=[pl.BlockSpec(memory_space=pltpu.VMEM)] * 3,
        out_specs=pl.BlockSpec((2, inputs, inputs), lambda i: (i, 0, 0)),
        out_shape=jax.ShapeDtypeStruct((channels, inputs, inputs), BF16),
        scratch_shapes=[pltpu.VMEM(arrived.shape, F32)],
        interpret=interpret,
        compiler_params=pltpu.CompilerParams(vmem_limit_bytes=24 << 20),
        name="correlate",
    )(arrived, sel, inv)


def tile_kernel(flag_ref, row_ref, o_ref):
    own, n = flag_ref.shape
    down = lax.broadcasted_iota(jnp.int32, (own, n), 0)
    ids = jnp.zeros((own, n), jnp.int32)
    for q in range(own):
        ids = jnp.where(down == q, row_ref[q], ids)
    block = jnp.concatenate([flag_ref[...], ids.astype(F32)], axis=0)
    for d in range(o_ref.shape[0]):
        o_ref[d] = block


def make_tiles(flags, station_row, copies, interpret=False):
    return pl.pallas_call(
        tile_kernel,
        out_shape=jax.ShapeDtypeStruct((copies, 2 * flags.shape[0], flags.shape[1]), F32),
        in_specs=[pl.BlockSpec(memory_space=pltpu.VMEM), pl.BlockSpec(memory_space=pltpu.SMEM)],
        interpret=interpret,
        name="make_tiles",
    )(flags, station_row)


def gather_line(tile, axis):
    parts = [tile]
    for shift in range(1, 4):
        parts.append(lax.ppermute(tile, axis, [(i, (i + shift) % 4) for i in range(4)]))
    return jnp.concatenate(parts, axis=0)


def on_device(voltages, flags, station_row):
    spectra = flags.shape[1]
    z_hi = (2 * lax.axis_index("a") + lax.axis_index("b")).astype(jnp.int32).reshape(1)
    frames = jnp.transpose(voltages[0].reshape(2, -1, 16, 128), (1, 2, 0, 3)).reshape(-1, 128)
    tile = make_tiles(flags, station_row, 4)
    tile = lax.all_to_all(tile, "l", split_axis=0, concat_axis=0, tiled=True).reshape(32, spectra)
    blocks = channelize(frames, flags, z_hi, spectra).reshape(512, 8, spectra)
    tile, blocks = lax.optimization_barrier((tile, blocks))
    moved = lax.all_to_all(blocks, ("c", "a", "b", "l", "x", "y"), split_axis=0, concat_axis=0, tiled=True)
    for axis in ("x", "y"):
        tile = gather_line(tile, axis)
    place = jnp.stack([lax.axis_index(axis) for axis in ("x", "y")]).astype(jnp.int32)
    sel, inv = prepare(tile, place, 512)
    return correlate(moved.reshape(4096, spectra), sel, inv)


def solution(mesh):
    axes = ("x", "l", "y", "a", "b", "c")
    fine = jax.sharding.Mesh(mesh.devices.reshape(4, 4, 4, 2, 2, 2), axes)
    stn = axes[:3]
    return jax.shard_map(
        on_device,
        mesh=fine,
        in_specs=(P(axes, None, None, None), P(stn, None), P(stn)),
        out_specs=P(axes, None, None),
        check_vma=False,
    )
```
